32 devices in a mesh: dp: 4 (over x, core), ctx: 8 (over z, y).
Axes of the slice: x: 2, y: 2, z: 4, core: 2. Of those that a mesh axis runs over, the one named last changes fastest.
Arguments:
- activations: bfloat16 [640, 4096], P('ctx', 'dp'), may hold values from -6 to 6
- queries: bfloat16 [640, 16, 128], P('ctx', 'dp'), may hold values from -300 to 300
- w_kv: bfloat16 [4096, 4, 2, 128], P(('dp', 'ctx')), may hold values from -0.09375 to 0.09375
- span_of: int32 [16], P('ctx'), may hold values from 0 to 15, as said below
Outputs:
- attended: bfloat16 [640, 2048], P('ctx', 'dp')
The draws below stay inside these ranges and needn't reach their ends.
Inputs may be any that keep to these rules, and one draw needn't show every extreme that they name: `span_of`: each span number appears once. The two slots of one ctx index hold spans c and 2 * 8 - 1 - c for some c, in either order.
All inputs are finite; a program needn't handle non-finite values.
Results may differ from the reference program's by a relative error of at most 0.0066.
Values may be sent and summed in bfloat16 or wider, within the bound.
A program may use at most 64 MiB of HBM per device.

```python
import math
import jax
import jax.numpy as jnp
from jax import lax

D = 4096
HD = 128
GROUP = 4
KV_HEADS = 4
Q_HEADS = 16
SPAN = 40
SEQ = 640
N_CTX = 8


def span_table(key):
    pairs = jax.random.permutation(jax.random.fold_in(key, 201), N_CTX).astype(jnp.int32)
    flips = jax.random.randint(jax.random.fold_in(key, 202), (N_CTX,), 0, 2).astype(jnp.int32)
    upper = 2 * N_CTX - 1 - pairs
    first = jnp.where(flips == 1, upper, pairs)
    second = jnp.where(flips == 1, pairs, upper)
    return jnp.stack([first, second], axis=1).reshape(2 * N_CTX).astype(jnp.int32)


def base_inputs(key):
    inner = jax.random.fold_in(key, 101)
    return jnp.clip(jax.random.normal(inner, (SEQ, D), jnp.float32), -6.0, 6.0)


def base_w(key):
    inner = jax.random.fold_in(key, 102)
    raw = jnp.clip(jax.random.normal(inner, (D, KV_HEADS, 2, HD), jnp.float32), -6.0, 6.0)
    return raw * (1.0 / math.sqrt(D))


def draw_span_of(key, part):
    return span_table(key)


def draw_activations(key, part):
    return base_inputs(key).astype(jnp.bfloat16)


def draw_w_kv(key, part):
    return base_w(key).astype(jnp.bfloat16)


def draw_queries(key, part):
    inner = jax.random.fold_in(key, 103)
    query = jnp.clip(jax.random.normal(inner, (SEQ, Q_HEADS, HD), jnp.float32), -6.0, 6.0)
    return query.astype(jnp.bfloat16)


def setup_inputs(seed: int = 0) -> dict:
    key_of = jax.random.split(jax.random.key(seed), 5)
    activations = draw_activations(jax.random.fold_in(key_of[4], 71), 0)
    queries = draw_queries(jax.random.fold_in(key_of[4], 71), 0)
    w_kv = draw_w_kv(jax.random.fold_in(key_of[4], 71), 0)
    span_of = draw_span_of(jax.random.fold_in(key_of[4], 71), 0)
    return {"activations": activations, "queries": queries, "w_kv": w_kv, "span_of": span_of}


def reference(activations, queries, w_kv, span_of):
    rows = jnp.arange(SEQ, dtype=jnp.int32)
    position = (jnp.take(span_of, rows // SPAN) * SPAN + rows % SPAN).astype(jnp.int32)
    flat = w_kv.reshape(D, KV_HEADS * 2 * HD)
    key_value = jnp.dot(activations, flat, preferred_element_type=jnp.float32).astype(jnp.bfloat16)
    key_value = key_value.reshape(SEQ, KV_HEADS, 2, HD)
    visible = position[None, :] <= position[:, None]
    scale = 1.0 / math.sqrt(HD)

    def one_head(head):
        query = lax.dynamic_index_in_dim(queries, head, 1, keepdims=False).astype(jnp.float32)
        pair = lax.dynamic_index_in_dim(key_value, head // GROUP, 1, keepdims=False)
        keys = pair[:, 0].astype(jnp.float32)
        values = pair[:, 1]
        score = jnp.dot(query, keys.T, precision=lax.Precision.HIGHEST) * scale
        top = lax.optimization_barrier(jnp.max(jnp.where(visible, score, -1e+30), axis=1, keepdims=True))
        weight = jnp.where(visible, jnp.exp(score - top), 0.0)
        total = lax.optimization_barrier(jnp.sum(weight, axis=1, keepdims=True))
        mixed = jnp.dot(weight.astype(jnp.bfloat16), values, preferred_element_type=jnp.float32) / total
        return mixed.astype(jnp.bfloat16)
    heads_out = lax.map(one_head, jnp.arange(Q_HEADS, dtype=jnp.int32))
    return jnp.transpose(heads_out, (1, 0, 2)).reshape(SEQ, Q_HEADS * HD)
```

```python
import functools
import math

import jax
import jax.numpy as jnp
from jax import lax
from jax.experimental import pallas as pl
from jax.experimental.pallas import tpu as pltpu
from jax.sharding import PartitionSpec as P

MESH = pl.DeviceIdType.MESH
VALUE_PART = jnp.bfloat16
PIECES = 1


def remote(src, dst, send, recv, dp, ctx):
    return pltpu.make_async_remote_copy(
        src_ref=src,
        dst_ref=dst,
        send_sem=send,
        recv_sem=recv,
        device_id={"dp": dp, "ctx": ctx},
        device_id_type=MESH,
    )


def fused_kernel(
    X, C, Z, G, scale,
    a_ref, q_in, w_hbm, span_ref, o_ref,
    q_ref, w_in, wloc, abuf, wbuf,
    pk, ck, sk, rk, kbuf, pv, cv, sv, rv, vbuf, spbuf,
    az_s, az_r, ax_s, ax_r, wx_s, wx_r, wy_s, wy_r, co_s, co_r,
    rz_s, rz_r, kz_s, kz_r, ky_s, ky_r, sz_s, sz_r, sy_s, sy_r, own_s,
):
    dp, ctx = lax.axis_index("dp"), lax.axis_index("ctx")
    x, c = lax.div(dp, C), lax.rem(dp, C)
    z, y = lax.div(ctx, G), lax.rem(ctx, G)
    tokens = a_ref.shape[0]
    half = tokens // 2
    fw, nw = abuf.shape[3], wbuf.shape[3]
    hw = nw // C
    hd = hw // 2
    cut = w_in.shape[0] // PIECES
    pieces = [pl.ds(i * cut, cut) for i in range(PIECES)]

    def ahead(i, k, n):
        return lax.rem(i + k, n)

    def behind(i, k, n):
        return lax.rem(i + (n - k), n)

    way = 1 - 2 * lax.div(2 * z, Z)

    def along(k):
        return lax.rem(z + way * k + Z, Z) if k else z

    def arrived(slot, recv):
        remote(slot, slot, recv, recv, dp, ctx).wait_recv()

    sent = []

    def send(*args):
        copy = remote(*args)
        copy.start()
        sent.append(copy)

    peers = [(dp, along(k) * G + y) for k in range(1, Z)]
    peers += [(dp, z * G + ahead(y, k, G)) for k in range(1, G)]
    peers += [(ahead(x, k, X) * C + c, ctx) for k in range(1, X)]
    peers += [(x * C + ahead(c, k, C), ctx) for k in range(1, C)]
    load_w = pltpu.make_async_copy(w_hbm, w_in, own_s.at[2])
    load_q = pltpu.make_async_copy(q_in, q_ref, own_s.at[3])
    barrier = pltpu.get_barrier_semaphore()
    for pd, pc in peers:
        pl.semaphore_signal(barrier, inc=1, device_id={"dp": pd, "ctx": pc}, device_id_type=MESH)
    spbuf[ctx] = jnp.where(
        lax.broadcasted_iota(jnp.int32, spbuf.shape[1:], 0) == 0, span_ref[0], span_ref[1]
    )
    load_w.start()
    load_q.start()
    w_ref = wloc
    pl.semaphore_wait(barrier, len(peers))

    for k in range(Z - 1, 0, -1):
        zt = along(k)
        send(a_ref.at[:, pl.ds(pl.multiple_of(zt * fw, fw), fw)], abuf.at[x, z],
             az_s.at[k], az_r.at[z], dp, zt * G + y)
    load_w.wait()
    for h in range(w_in.shape[1]):
        for i in range(2):
            wloc[:, (2 * h + i) * hd:(2 * h + i + 1) * hd] = w_in[:, h, i, :]
    own_a = a_ref.at[:, pl.ds(pl.multiple_of(z * fw, fw), fw)]
    own_w = w_ref.at[:, pl.ds(pl.multiple_of(x * nw, nw), nw)]
    for k in range(1, X):
        xt = ahead(x, k, X)
        for i, part in enumerate(pieces):
            send(w_ref.at[part, pl.ds(pl.multiple_of(xt * nw, nw), nw)], wbuf.at[x, y, part],
                 wx_s.at[k, i], wx_r.at[k, i], xt * C + c, ctx)
        send(own_a, abuf.at[x, z], ax_s.at[k, 0], ax_r.at[k, z], xt * C + c, ctx)
    for k in range(1, G):
        for i, part in enumerate(pieces):
            send(own_w.at[part], wbuf.at[x, y, part], wy_s.at[0, k, i], wy_r.at[0, k, i],
                 dp, z * G + ahead(y, k, G))
    copy_a = pltpu.make_async_copy(own_a, abuf.at[x, z], own_s.at[0])
    copy_w = pltpu.make_async_copy(own_w, wbuf.at[x, y], own_s.at[1])
    copy_a.start()
    copy_w.start()
    for k in range(1, Z):
        send(spbuf.at[ctx], spbuf.at[ctx], sz_s.at[k], sz_r.at[z], dp, along(k) * G + y)
    for g in range(1, G):
        send(spbuf.at[ctx], spbuf.at[ctx], sy_s.at[g, 0], sy_r.at[g, 0], dp, z * G + ahead(y, g, G))

    def relay_w(i):
        for k in range(1, X):
            slot = wbuf.at[behind(x, k, X), y, pieces[i]]
            arrived(slot, wx_r.at[k, i])
            for g in range(1, G):
                send(slot, slot, wy_s.at[k, g, i], wy_r.at[k, g, i], dp, z * G + ahead(y, g, G))

    def relay_a(k):
        zs = along(k)
        arrived(abuf.at[x, zs], az_r.at[zs])
        for j in range(1, X):
            send(abuf.at[x, zs], abuf.at[x, zs], ax_s.at[j, k], ax_r.at[j, zs], ahead(x, j, X) * C + c, ctx)

    for i in range(max(len(pieces), Z - 1)):
        if i < len(pieces):
            relay_w(i)
        if i < Z - 1:
            relay_a(i + 1)
    for k in range(1, Z):
        src = along(k) * G + y
        arrived(spbuf.at[src], sz_r.at[along(k)])
        for g in range(1, G):
            send(spbuf.at[src], spbuf.at[src], sy_s.at[g, k], sy_r.at[g, k], dp, z * G + ahead(y, g, G))

    copy_a.wait()
    copy_w.wait()
    for k in range(X):
        xs = behind(x, k, X)
        for g in range(1, G):
            for i, part in enumerate(pieces):
                arrived(wbuf.at[xs, behind(y, g, G), part], wy_r.at[k, g, i])
        if k:
            for j in range(Z):
                arrived(abuf.at[xs, along(j)], ax_r.at[k, along(j)])
        rows = abuf[xs].reshape(Z * tokens, fw)
        weights = wbuf[xs].reshape(fw, nw)
        part = jnp.dot(rows, weights, preferred_element_type=jnp.float32)
        held = held + part if k else part
    for h in range(C):
        pk[h] = held[:, h * hw:h * hw + hd].reshape(Z, tokens, hd)
        pv[h] = held[:, h * hw + hd:(h + 1) * hw].reshape(Z, tokens, hd).astype(pv.dtype)
    keys_of, values_of = (pk, ck, sk, rk, kbuf), (pv, cv, sv, rv, vbuf)

    order = [k for k in range(Z - 1, 0, -1)] + [0]
    parts, others, sums, incoming, outs = zip(keys_of, values_of)
    for i in range(2):
        for k in order:
            zt = along(k)
            for j in range(1, C):
                ct = ahead(c, j, C)
                send(parts[i].at[ct, zt], others[i].at[j, zt], co_s.at[i, j, k], co_r.at[i, j, k], x * C + ct, ctx)
    totals = [None, None]
    for i in range(2):
        for k in order:
            zt = along(k)
            part = parts[i][c, zt].astype(jnp.float32)
            for j in range(1, C):
                arrived(others[i].at[j, zt], co_r.at[i, j, k])
                part += others[i][j, zt].astype(jnp.float32)
            if k:
                sums[i][k] = part.astype(sums[i].dtype)
                send(sums[i].at[k], incoming[i].at[z], rz_s.at[i, k], rz_r.at[i, z], dp, zt * G + y)
            else:
                totals[i] = part

    for i in range(2):
        for k in range(1, Z):
            zs = along(k)
            arrived(incoming[i].at[zs], rz_r.at[i, zs])
            totals[i] += incoming[i][zs].astype(jnp.float32)
        outs[i][ctx] = totals[i].astype(outs[i].dtype)
        mine = outs[i].at[ctx]
        for k in range(Z - 1, 0, -1):
            send(mine, mine, kz_s.at[i, k], kz_r.at[i, z], dp, along(k) * G + y)
        for g in range(1, G):
            send(mine, mine, ky_s.at[i, g, 0], ky_r.at[i, g, 0], dp, z * G + ahead(y, g, G))

    for k in range(Z):
        for g in range(1, G):
            src = along(k) * G + behind(y, g, G)
            arrived(spbuf.at[src], sy_r.at[g, k])
    count = Z * G * tokens
    lane = lax.broadcasted_iota(jnp.int32, (1, count), 1)
    key_pos = jnp.zeros((1, count), jnp.int32)
    lanes = spbuf.shape[2]
    for j in range(Z * G):
        for i in range(2):
            base = j * tokens + i * half
            row = spbuf[j, i:i + 1, :]
            row = jnp.concatenate([row] * (count // lanes), axis=1)
            key_pos = jnp.where((lane >= base) & (lane < base + half), row * half + (lane - base), key_pos)
    at = lax.broadcasted_iota(jnp.int32, (tokens, 1), 0)
    own_pos = jnp.where(at < half, span_ref[0] * half + at, span_ref[1] * half + (at - half))
    visible = key_pos <= own_pos

    def relay(i):
        for k in range(1, Z):
            zs = along(k)
            slot = outs[i].at[zs * G + y]
            arrived(slot, kz_r.at[i, zs])
            for g in range(1, G):
                send(slot, slot, ky_s.at[i, g, k], ky_r.at[i, g, k], dp, z * G + ahead(y, g, G))

    def gathered(i):
        for k in range(Z):
            for g in range(1, G):
                arrived(outs[i].at[along(k) * G + behind(y, g, G)], ky_r.at[i, g, k])

    load_q.wait()
    relay(0)
    relay(1)
    gathered(0)
    keys = outs[0][...].reshape(count, hd)
    heads = range(q_ref.shape[1])
    weights, norms = [], []
    for g in heads:
        query = q_ref[:, g, :]
        score = lax.dot_general(query, keys, (((1,), (1,)), ((), ())), preferred_element_type=jnp.float32)
        score = jnp.where(visible, score * scale, -1e30)
        top = jnp.max(score, axis=1, keepdims=True)
        weight = jnp.where(visible, jnp.exp(score - top), 0.0)
        norms.append(jnp.sum(weight, axis=1, keepdims=True))
        weights.append(weight.astype(jnp.bfloat16))
    gathered(1)
    values = outs[1][...].reshape(count, hd)
    for g in heads:
        mixed = jnp.dot(weights[g], values, preferred_element_type=jnp.float32)
        o_ref[:, g * hd:(g + 1) * hd] = (mixed / norms[g]).astype(o_ref.dtype)

    for copy in sent:
        copy.wait_send()


def plan(mesh, tokens, shard_rows, heads, head_dim):
    dp, ctx = mesh.shape["dp"], mesh.shape["ctx"]
    if heads != dp or tokens % 16 or shard_rows % (16 * PIECES) or head_dim % 128 or (ctx * tokens) % 128:
        return None
    C = 2 if dp % 2 == 0 else 1
    G = 2 if ctx % 2 == 0 else 1
    if (G * shard_rows) % 128 or ctx > 16:
        return None
    return dp // C, C, ctx // G, G


def fused(factors, activations, queries, w_kv, span_of):
    X, C, Z, G = factors
    tokens = activations.shape[0]
    shard_rows, heads, _, hd = w_kv.shape
    hw, fw, ctx = 2 * hd, G * shard_rows, Z * G
    nw = C * hw
    group = queries.shape[1]
    dma = pltpu.SemaphoreType.DMA
    bf16, f32 = jnp.bfloat16, jnp.float32
    pair = lambda *shape: [dma(shape), dma(shape)]

    def scratch(dtype):
        block = (tokens, hd)
        full, part = pltpu.VMEM((C, Z, *block), f32), pltpu.VMEM((Z, *block), dtype)
        return [full, full, part, part] + [pltpu.VMEM((ctx, *block), bf16)]

    hbm = pl.BlockSpec(memory_space=pl.ANY)
    vmem = pl.BlockSpec(memory_space=pltpu.VMEM)
    return pl.pallas_call(
        functools.partial(fused_kernel, X, C, Z, G, 1.0 / math.sqrt(hd)),
        out_shape=pltpu.VMEM((tokens, group * hd), bf16),
        in_specs=[hbm, hbm, hbm, pl.BlockSpec(memory_space=pltpu.SMEM)],

        scratch_shapes=[
            pltpu.VMEM(queries.shape, bf16),
            pltpu.VMEM(w_kv.shape, bf16),
            pltpu.VMEM((shard_rows, heads * hw), bf16),
            pltpu.VMEM((X, Z, tokens, fw), bf16),
            pltpu.VMEM((X, G, shard_rows, nw), bf16),
            *scratch(f32), *scratch(VALUE_PART),
            pltpu.VMEM((ctx, 8, 128), jnp.int32),
            *pair(Z), *pair(X, Z), *pair(X, PIECES), *pair(X, G, PIECES), *pair(2, C, Z),
            *pair(2, Z), *pair(2, Z), *pair(2, G, Z), *pair(Z), *pair(G, Z),
            dma((4,)),
        ],
        compiler_params=pltpu.CompilerParams(collective_id=0, has_side_effects=True),
        name="fused",
    )(
        activations,
        queries,
        w_kv,
        span_of,
    )


def attend(carry, keys, values, key_pos, query, query_pos, scale):
    top, total, accum = carry
    score = jnp.einsum("tgd,nd->tgn", query, keys, preferred_element_type=jnp.float32) * scale
    visible = (key_pos[None, :] <= query_pos[:, None])[:, None, :]
    new_top = jnp.maximum(top, jnp.max(jnp.where(visible, score, -1e30), axis=2))
    weight = jnp.where(visible, jnp.exp(score - new_top[..., None]), 0.0)
    factor = jnp.exp(top - new_top)
    total = total * factor + jnp.sum(weight, axis=2)
    accum = accum * factor[..., None] + jnp.einsum(
        "tgn,nd->tgd", weight.astype(jnp.bfloat16), values, preferred_element_type=jnp.float32
    )
    return (new_top, total, accum)


def body(activations, queries, w_kv, span_of, mesh=None):
    factors = plan(mesh, activations.shape[0], w_kv.shape[0], w_kv.shape[1], queries.shape[2])
    if factors is not None:
        return fused(factors, activations, queries, w_kv, span_of)
    tokens = activations.shape[0]
    head_dim = queries.shape[2]
    half = tokens // 2
    scale = 1.0 / math.sqrt(head_dim)
    whole = lax.all_gather(activations, "dp", axis=1, tiled=True)
    shard_rows = w_kv.shape[0]
    mine = lax.all_to_all(w_kv, "dp", split_axis=1, concat_axis=0, tiled=True)
    ordered = whole.reshape(tokens, lax.axis_size("dp"), lax.axis_size("ctx"), shard_rows)
    ordered = jnp.transpose(ordered, (0, 2, 1, 3)).reshape(tokens, -1)
    piece = lax.all_gather(mine, "ctx", axis=0, tiled=True)
    count = piece.shape[0]
    projected = jnp.dot(ordered, piece.reshape(count, -1), preferred_element_type=jnp.float32)
    key_value = projected.astype(jnp.bfloat16).reshape(tokens, 2, head_dim)
    all_spans = lax.all_gather(span_of, "ctx", axis=0, tiled=True)
    offsets = jnp.arange(tokens, dtype=jnp.int32)
    own_pos = jnp.where(offsets < half, span_of[0], span_of[1]) * half + offsets % half

    def update(state, part, part_pos):
        return attend(state, part[:, 0], part[:, 1], part_pos, queries, own_pos, scale)

    group = queries.shape[1]
    start_state = (
        jnp.full((tokens, group), -1e30, jnp.float32),
        jnp.zeros((tokens, group), jnp.float32),
        jnp.zeros((tokens, group, head_dim), jnp.float32),
    )
    state = start_state
    piece = lax.all_gather(key_value, "ctx", axis=0, tiled=True)
    count = piece.shape[0]
    index = jnp.arange(count, dtype=jnp.int32)
    key_pos = jnp.take(all_spans, index // half) * half + index % half
    block = 1024 if count % 1024 == 0 else count

    def step(held, item):
        return (update(held, item[0], item[1]), None)

    blocks = (
        piece.reshape(count // block, block, 2, head_dim),
        key_pos.reshape(count // block, block),
    )
    state, _ = lax.scan(step, state, blocks)
    top, total, accum = state
    return (accum / total[..., None]).astype(jnp.bfloat16).reshape(tokens, group * head_dim)


def solution(mesh):
    return jax.shard_map(
        functools.partial(body, mesh=mesh),
        mesh=mesh,
        in_specs=(
            P("ctx", "dp"),
            P("ctx", "dp", None),
            P(("dp", "ctx"), None, None, None),
            P("ctx"),
        ),
        out_specs=P("ctx", "dp"),
        check_vma=False,
    )
```

```python
import functools
import math

import jax
import jax.numpy as jnp
from jax import lax
from jax.experimental import pallas as pl
from jax.experimental.pallas import tpu as pltpu
from jax.sharding import PartitionSpec as P

MESH = pl.DeviceIdType.MESH
VALUE_PART = jnp.bfloat16


def remote(src, dst, send, recv, dp, ctx):
    return pltpu.make_async_remote_copy(
        src_ref=src,
        dst_ref=dst,
        send_sem=send,
        recv_sem=recv,
        device_id={"dp": dp, "ctx": ctx},
        device_id_type=MESH,
    )


def fused_kernel(
    X, C, Z, G, scale,
    a_ref, q_in, w_hbm, span_ref, o_ref,
    q_ref, w_in, wloc, abuf, wbuf, psum_k, psum_v, got_k, got_v, kbuf, vbuf, spbuf, bias,
    send_sem, a_sem, w_sem, p_sem, g_sem, s_sem, own_sem,
):
    dp, ctx = lax.axis_index("dp"), lax.axis_index("ctx")
    x, c = lax.div(dp, C), lax.rem(dp, C)
    z, y = lax.div(ctx, G), lax.rem(ctx, G)
    tokens = a_ref.shape[0]
    half = tokens // 2
    fw, hd = abuf.shape[3], kbuf.shape[2]
    heads = w_in.shape[1]
    psum, got, outs = (psum_k, psum_v), (got_k, got_v), (kbuf, vbuf)
    xo, co, yo = X - 1 - x, C - 1 - c, G - 1 - y
    across, beside, corner = xo * C + c, x * C + co, xo * C + co

    way = 1 - 2 * lax.div(2 * z, Z)
    edge = (z == 0) | (z == Z - 1)
    line = [z, z + way, jnp.where(edge, z + 2 * way, z - way), jnp.where(edge, z + 3 * way, z + 2 * way)]

    def arrived(slot, recv):
        remote(slot, slot, recv, recv, dp, ctx).wait_recv()

    sent = []

    def send(src, dst, recv, to_dp, to_ctx):
        copy = remote(src, dst, send_sem.at[len(sent)], recv, to_dp, to_ctx)
        sent.append((copy, None))
        copy.start()

    def send_if(want, src, dst, recv, to_dp, to_ctx):
        copy = remote(src, dst, send_sem.at[len(sent)], recv, to_dp, to_ctx)
        sent.append((copy, want))
        pl.when(want)(copy.start)

    peers = [(dp, line[k] * G + y) for k in range(1, Z)]
    peers += [(dp, line[k] * G + yo) for k in range(Z)]
    peers += [(beside, z * G + yo), (across, ctx), (beside, ctx), (corner, ctx)]
    load_w = pltpu.make_async_copy(w_hbm, w_in, own_sem.at[2])
    load_q = pltpu.make_async_copy(q_in, q_ref, own_sem.at[3])
    barrier = pltpu.get_barrier_semaphore()
    for pd, pc in peers:
        pl.semaphore_signal(barrier, inc=1, device_id={"dp": pd, "ctx": pc}, device_id_type=MESH)
    load_w.start()
    own_a = a_ref.at[:, pl.ds(pl.multiple_of(z * fw, fw), fw)]
    copy_a = pltpu.make_async_copy(own_a, abuf.at[dp, z], own_sem.at[0])
    copy_a.start()
    load_q.start()
    spbuf[ctx] = jnp.where(
        lax.broadcasted_iota(jnp.int32, spbuf.shape[1:], 0) == 0, span_ref[0], span_ref[1]
    )
    pl.semaphore_wait(barrier, len(peers))

    for k in range(1, Z):
        zt = line[k]
        send(a_ref.at[:, pl.ds(pl.multiple_of(zt * fw, fw), fw)], abuf.at[dp, z],
             a_sem.at[dp, z], dp, zt * G + y)
    send(own_a, abuf.at[dp, z], a_sem.at[dp, z], across, ctx)
    send(own_a, abuf.at[dp, z], a_sem.at[dp, z], beside, ctx)
    load_w.wait()
    for i in range(2):
        for h in range(heads):
            wloc[i, h] = w_in[:, h, i, :]
        slot, recv = wbuf.at[i, dp, y], w_sem.at[i, dp, y]
        for h in (across, corner):
            send(wloc.at[i, h], slot, recv, h, ctx)
        for h in (dp, beside):
            send(wloc.at[i, h], slot, recv, h, z * G + yo)
        send(wloc.at[i, beside], slot, recv, beside, ctx)
        wbuf[i, dp, y] = wloc[i, dp]
    for k in range(Z):
        if k:
            send(spbuf.at[ctx], spbuf.at[ctx], s_sem.at[ctx], dp, line[k] * G + y)
        send(spbuf.at[ctx], spbuf.at[ctx], s_sem.at[ctx], dp, line[k] * G + yo)

    def relay_w(i):
        for d in (across, corner):
            slot, recv = wbuf.at[i, d, y], w_sem.at[i, d, y]
            arrived(slot, recv)
            send(slot, slot, recv, dp, z * G + yo)

    def relay_z(k):
        slot, recv = abuf.at[dp, line[k]], a_sem.at[dp, line[k]]
        arrived(slot, recv)
        send(slot, slot, recv, across, ctx)
        send(slot, slot, recv, beside, ctx)

    def relay_x(k):
        slot, recv = abuf.at[across, line[k]], a_sem.at[across, line[k]]
        arrived(slot, recv)
        send(slot, slot, recv, beside, ctx)

    def project(i, k):
        rows = [abuf[d, line[k]] for d in range(X * C)]
        held = None
        for d in range(X * C):
            part = jnp.dot(rows[d], wbuf[i, d].reshape(fw, hd), preferred_element_type=jnp.float32)
            held = part if held is None else held + part
        return held

    def share(i, k):
        if i == 0:
            for d in (beside, corner):
                arrived(abuf.at[d, line[k]], a_sem.at[d, line[k]])
        if k:
            psum[i][line[k]] = project(i, k).astype(psum[i].dtype)
            send(psum[i].at[line[k]], got[i].at[z], p_sem.at[i, z], dp, line[k] * G + y)

    def columns(i):
        arrived(wbuf.at[i, beside, y], w_sem.at[i, beside, y])
        for d in (dp, beside, across, corner):
            arrived(wbuf.at[i, d, yo], w_sem.at[i, d, yo])

    relay_z(1)
    relay_x(0)
    relay_z(2)
    relay_w(0)
    relay_z(3)
    relay_x(1)
    relay_w(1)
    relay_x(2)
    relay_x(3)
    columns(0)
    for k in range(1, Z):
        share(0, k)
    columns(1)
    for k in range(1, Z):
        share(1, k)
    copy_a.wait()
    share(0, 0)
    totals = [project(0, 0), project(1, 0)]

    for k in range(Z):
        if k:
            arrived(spbuf.at[line[k] * G + y], s_sem.at[line[k] * G + y])
        arrived(spbuf.at[line[k] * G + yo], s_sem.at[line[k] * G + yo])
    count = Z * G * tokens
    lane = lax.broadcasted_iota(jnp.int32, (1, count), 1)
    key_pos = jnp.zeros((1, count), jnp.int32)
    lanes = spbuf.shape[2]
    for j in range(Z * G):
        for i in range(2):
            base = j * tokens + i * half
            row = spbuf[j, i:i + 1, :]
            row = jnp.concatenate([row] * (count // lanes), axis=1)
            key_pos = jnp.where((lane >= base) & (lane < base + half), row * half + (lane - base), key_pos)
    at = lax.broadcasted_iota(jnp.int32, (tokens, 1), 0)
    own_pos = jnp.where(at < half, span_ref[0] * half + at, span_ref[1] * half + (at - half))
    bias[...] = jnp.where(key_pos <= own_pos, 0.0, -1e30)

    def straight(source, target):
        return (lax.div(2 * source, Z) == lax.div(2 * target, Z)) | (target == 0)

    for i in range(2):
        for k in range(1, Z):
            zs = line[k]
            arrived(got[i].at[zs], p_sem.at[i, zs])
            totals[i] += got[i][zs].astype(jnp.float32)
        outs[i][ctx] = totals[i].astype(outs[i].dtype)
        mine, recv = outs[i].at[ctx], g_sem.at[i, ctx]
        for k in range(Z - 1, 0, -1):
            send(mine, mine, recv, dp, line[k] * G + y)
        send(mine, mine, recv, dp, z * G + yo)
        for k in range(Z - 1, 0, -1):
            send_if(straight(z, line[k]), mine, mine, recv, dp, line[k] * G + yo)

    def relay(i):
        for k in range(1, Z):
            src = line[k] * G + y
            slot, recv = outs[i].at[src], g_sem.at[i, src]
            arrived(slot, recv)
            send_if(jnp.logical_not(straight(line[k], z)), slot, slot, recv, dp, z * G + yo)

    def gathered(i):
        for k in range(Z):
            src = line[k] * G + yo
            arrived(outs[i].at[src], g_sem.at[i, src])

    load_q.wait()
    relay(0)
    relay(1)
    gathered(0)
    keys = outs[0][...].reshape(count, hd)
    weights, norms = [], []
    for g in range(q_ref.shape[1]):
        query = q_ref[:, g, :]
        score = lax.dot_general(query, keys, (((1,), (1,)), ((), ())), preferred_element_type=jnp.float32)
        score = score * scale + bias[...]
        weight = jnp.exp(score - jnp.max(score, axis=1, keepdims=True))
        norms.append(jnp.sum(weight, axis=1, keepdims=True))
        weights.append(weight.astype(jnp.bfloat16))
    gathered(1)
    values = outs[1][...].reshape(count, hd)
    for g in range(q_ref.shape[1]):
        mixed = jnp.dot(weights[g], values, preferred_element_type=jnp.float32)
        o_ref[:, g * hd:(g + 1) * hd] = (mixed / norms[g]).astype(o_ref.dtype)

    for copy, want in sent:
        if want is None:
            copy.wait_send()
        else:
            pl.when(want)(copy.wait_send)


def plan(mesh, tokens, shard_rows, heads, head_dim):
    dp, ctx = mesh.shape["dp"], mesh.shape["ctx"]
    if heads != dp or tokens % 16 or shard_rows % 16 or head_dim % 128 or (ctx * tokens) % 128:
        return None
    if dp != 4 or ctx != 8 or (2 * shard_rows) % 128:
        return None
    return dp // 2, 2, ctx // 2, 2


def fused(factors, activations, queries, w_kv, span_of):
    X, C, Z, G = factors
    tokens = activations.shape[0]
    shard_rows, heads, _, hd = w_kv.shape
    fw, ctx, dp = G * shard_rows, Z * G, X * C
    group = queries.shape[1]
    dma = pltpu.SemaphoreType.DMA
    bf16, f32 = jnp.bfloat16, jnp.float32
    block = (tokens, hd)
    hbm = pl.BlockSpec(memory_space=pl.ANY)
    sends = 20 * Z + 40
    return pl.pallas_call(
        functools.partial(fused_kernel, X, C, Z, G, 1.0 / math.sqrt(hd)),
        out_shape=pltpu.VMEM((tokens, group * hd), bf16),
        in_specs=[hbm, hbm, hbm, pl.BlockSpec(memory_space=pltpu.SMEM)],
        scratch_shapes=[
            pltpu.VMEM(queries.shape, bf16),
            pltpu.VMEM(w_kv.shape, bf16),
            pltpu.VMEM((2, heads, shard_rows, hd), bf16),
            pltpu.VMEM((dp, Z, tokens, fw), bf16),
            pltpu.VMEM((2, dp, G, shard_rows, hd), bf16),
            pltpu.VMEM((Z, *block), f32),
            pltpu.VMEM((Z, *block), VALUE_PART),
            pltpu.VMEM((Z, *block), f32),
            pltpu.VMEM((Z, *block), VALUE_PART),
            pltpu.VMEM((ctx, *block), bf16),
            pltpu.VMEM((ctx, *block), bf16),
            pltpu.VMEM((ctx, 8, 128), jnp.int32),
            pltpu.VMEM((tokens, ctx * tokens), f32),
            dma((sends,)), dma((dp, Z)), dma((2, dp, G)), dma((2, Z)), dma((2, ctx)), dma((ctx,)), dma((4,)),
        ],
        compiler_params=pltpu.CompilerParams(collective_id=0, has_side_effects=True),
        name="fused",
    )(
        activations,
        queries,
        w_kv,
        span_of,
    )


def attend(carry, keys, values, key_pos, query, query_pos, scale):
    top, total, accum = carry
    score = jnp.einsum("tgd,nd->tgn", query, keys, preferred_element_type=jnp.float32) * scale
    visible = (key_pos[None, :] <= query_pos[:, None])[:, None, :]
    new_top = jnp.maximum(top, jnp.max(jnp.where(visible, score, -1e30), axis=2))
    weight = jnp.where(visible, jnp.exp(score - new_top[..., None]), 0.0)
    factor = jnp.exp(top - new_top)
    total = total * factor + jnp.sum(weight, axis=2)
    accum = accum * factor[..., None] + jnp.einsum(
        "tgn,nd->tgd", weight.astype(jnp.bfloat16), values, preferred_element_type=jnp.float32
    )
    return (new_top, total, accum)


def body(activations, queries, w_kv, span_of, mesh=None):
    factors = plan(mesh, activations.shape[0], w_kv.shape[0], w_kv.shape[1], queries.shape[2])
    if factors is not None:
        return fused(factors, activations, queries, w_kv, span_of)
    tokens = activations.shape[0]
    head_dim = queries.shape[2]
    half = tokens // 2
    scale = 1.0 / math.sqrt(head_dim)
    whole = lax.all_gather(activations, "dp", axis=1, tiled=True)
    shard_rows = w_kv.shape[0]
    mine = lax.all_to_all(w_kv, "dp", split_axis=1, concat_axis=0, tiled=True)
    ordered = whole.reshape(tokens, lax.axis_size("dp"), lax.axis_size("ctx"), shard_rows)
    ordered = jnp.transpose(ordered, (0, 2, 1, 3)).reshape(tokens, -1)
    piece = lax.all_gather(mine, "ctx", axis=0, tiled=True)
    count = piece.shape[0]
    projected = jnp.dot(ordered, piece.reshape(count, -1), preferred_element_type=jnp.float32)
    key_value = projected.astype(jnp.bfloat16).reshape(tokens, 2, head_dim)
    all_spans = lax.all_gather(span_of, "ctx", axis=0, tiled=True)
    offsets = jnp.arange(tokens, dtype=jnp.int32)
    own_pos = jnp.where(offsets < half, span_of[0], span_of[1]) * half + offsets % half

    def update(state, part, part_pos):
        return attend(state, part[:, 0], part[:, 1], part_pos, queries, own_pos, scale)

    group = queries.shape[1]
    start_state = (
        jnp.full((tokens, group), -1e30, jnp.float32),
        jnp.zeros((tokens, group), jnp.float32),
        jnp.zeros((tokens, group, head_dim), jnp.float32),
    )
    state = start_state
    piece = lax.all_gather(key_value, "ctx", axis=0, tiled=True)
    count = piece.shape[0]
    index = jnp.arange(count, dtype=jnp.int32)
    key_pos = jnp.take(all_spans, index // half) * half + index % half
    block = 1024 if count % 1024 == 0 else count

    def step(held, item):
        return (update(held, item[0], item[1]), None)

    blocks = (
        piece.reshape(count // block, block, 2, head_dim),
        key_pos.reshape(count // block, block),
    )
    state, _ = lax.scan(step, state, blocks)
    top, total, accum = state
    return (accum / total[..., None]).astype(jnp.bfloat16).reshape(tokens, group * head_dim)


def solution(mesh):
    return jax.shard_map(
        functools.partial(body, mesh=mesh),
        mesh=mesh,
        in_specs=(
            P("ctx", "dp"),
            P("ctx", "dp", None),
            P(("dp", "ctx"), None, None, None),
            P("ctx"),
        ),
        out_specs=P("ctx", "dp"),
        check_vma=False,
    )
```

```python
import functools
import math

import jax
import jax.numpy as jnp
from jax import lax
from jax.experimental import pallas as pl
from jax.experimental.pallas import tpu as pltpu
from jax.sharding import PartitionSpec as P

MESH = pl.DeviceIdType.MESH
VALUE_PART = jnp.bfloat16
STEPS = 32767.0


def remote(src, dst, send, recv, dp, ctx):
    return pltpu.make_async_remote_copy(
        src_ref=src,
        dst_ref=dst,
        send_sem=send,
        recv_sem=recv,
        device_id={"dp": dp, "ctx": ctx},
        device_id_type=MESH,
    )


def fused_kernel(
    X, C, Z, G, scale,
    a_ref, q_in, w_hbm, span_in, o_ref,
    q_ref, w_in, wloc, abuf, wbuf, psum_k, psum_v, got_k, got_v, rsum, rgot, kbuf, vbuf, spbuf, bias,
    send_sem, a_sem, w_sem, p_sem, r_sem, g_sem, s_sem, own_sem, span_ref,
):
    dp, ctx = lax.axis_index("dp"), lax.axis_index("ctx")
    x, c = lax.div(dp, C), lax.rem(dp, C)
    z, y = lax.div(ctx, G), lax.rem(ctx, G)
    tokens = a_ref.shape[0]
    half = tokens // 2
    fw, hd = abuf.shape[3], kbuf.shape[2]
    heads = w_in.shape[1]
    psum, got, outs = (psum_k, psum_v), (got_k, got_v), (kbuf, vbuf)
    xo, co, yo = X - 1 - x, C - 1 - c, G - 1 - y
    across, beside, corner = xo * C + c, x * C + co, xo * C + co

    way = 1 - 2 * lax.div(2 * z, Z)
    edge = (z == 0) | (z == Z - 1)
    line = [z, z + way, jnp.where(edge, z + 2 * way, z - way), jnp.where(edge, z + 3 * way, z + 2 * way)]

    def arrived(slot, recv):
        remote(slot, slot, recv, recv, dp, ctx).wait_recv()

    sent = []

    def send(src, dst, recv, to_dp, to_ctx):
        copy = remote(src, dst, send_sem.at[len(sent)], recv, to_dp, to_ctx)
        sent.append((copy, None))
        copy.start()

    def send_if(want, src, dst, recv, to_dp, to_ctx):
        copy = remote(src, dst, send_sem.at[len(sent)], recv, to_dp, to_ctx)
        sent.append((copy, want))
        pl.when(want)(copy.start)

    peers = [(dp, line[k] * G + y) for k in range(1, Z)]
    peers += [(dp, line[k] * G + yo) for k in range(Z)]
    peers += [(beside, z * G + yo), (across, ctx), (beside, ctx), (corner, ctx)]
    load_w = pltpu.make_async_copy(w_hbm, w_in, own_sem.at[2])
    load_q = pltpu.make_async_copy(q_in, q_ref, own_sem.at[3])
    barrier = pltpu.get_barrier_semaphore()
    for pd, pc in peers:
        pl.semaphore_signal(barrier, inc=1, device_id={"dp": pd, "ctx": pc}, device_id_type=MESH)
    load_s = pltpu.make_async_copy(span_in, span_ref, own_sem.at[1])
    load_w.start()
    load_s.start()
    own_a = a_ref.at[:, pl.ds(pl.multiple_of(z * fw, fw), fw)]
    copy_a = pltpu.make_async_copy(own_a, abuf.at[dp, z], own_sem.at[0])
    copy_a.start()
    load_q.start()
    pl.semaphore_wait(barrier, len(peers))

    for k in range(1, Z):
        zt = line[k]
        send(a_ref.at[:, pl.ds(pl.multiple_of(zt * fw, fw), fw)], abuf.at[dp, z],
             a_sem.at[dp, z], dp, zt * G + y)
    send(own_a, abuf.at[dp, z], a_sem.at[dp, z], across, ctx)
    send(own_a, abuf.at[dp, z], a_sem.at[dp, z], beside, ctx)
    load_w.wait()
    for i in range(2):
        for h in range(heads):
            wloc[i, h] = w_in[:, h, i, :]
        slot, recv = wbuf.at[i, dp, y], w_sem.at[i, dp, y]
        for h in (across, corner):
            send(wloc.at[i, h], slot, recv, h, ctx)
        for h in (dp, beside):
            send(wloc.at[i, h], slot, recv, h, z * G + yo)
        send(wloc.at[i, beside], slot, recv, beside, ctx)
        wbuf[i, dp, y] = wloc[i, dp]
    load_s.wait()
    spbuf[ctx] = jnp.where(
        lax.broadcasted_iota(jnp.int32, spbuf.shape[1:], 0) == 0, span_ref[0], span_ref[1]
    )
    for k in range(Z):
        if k:
            send(spbuf.at[ctx], spbuf.at[ctx], s_sem.at[ctx], dp, line[k] * G + y)
        send(spbuf.at[ctx], spbuf.at[ctx], s_sem.at[ctx], dp, line[k] * G + yo)

    def relay_w(i):
        for d in (across, corner):
            slot, recv = wbuf.at[i, d, y], w_sem.at[i, d, y]
            arrived(slot, recv)
            send(slot, slot, recv, dp, z * G + yo)

    def relay_z(k):
        slot, recv = abuf.at[dp, line[k]], a_sem.at[dp, line[k]]
        arrived(slot, recv)
        send(slot, slot, recv, across, ctx)
        send(slot, slot, recv, beside, ctx)

    def relay_x(k):
        slot, recv = abuf.at[across, line[k]], a_sem.at[across, line[k]]
        arrived(slot, recv)
        send(slot, slot, recv, beside, ctx)

    lanes = rsum.shape[2]
    diagonal = lax.broadcasted_iota(jnp.int32, (tokens, lanes), 0) == lax.broadcasted_iota(jnp.int32, (tokens, lanes), 1)

    def project(i, k):
        rows = [abuf[d, line[k]] for d in range(X * C)]
        held = None
        for d in range(X * C):
            part = jnp.dot(rows[d], wbuf[i, d].reshape(fw, hd), preferred_element_type=jnp.float32)
            held = part if held is None else held + part
        return held

    def share(i, k):
        if i == 0:
            for d in (beside, corner):
                arrived(abuf.at[d, line[k]], a_sem.at[d, line[k]])
        if k:
            part = project(i, k)
            if i == 0:
                peak = jnp.maximum(jnp.max(jnp.abs(part), axis=1, keepdims=True), 1e-30)
                part = jnp.round(part * (STEPS / peak)).astype(jnp.int32)
                peaks = jnp.sum(jnp.where(diagonal, peak, 0.0), axis=0, keepdims=True)
                rsum[line[k]] = jnp.broadcast_to(peaks, rsum.shape[1:])
                send(rsum.at[line[k]], rgot.at[z], r_sem.at[z], dp, line[k] * G + y)
            psum[i][line[k]] = part.astype(psum[i].dtype)
            send(psum[i].at[line[k]], got[i].at[z], p_sem.at[i, z], dp, line[k] * G + y)

    def columns(i):
        arrived(wbuf.at[i, beside, y], w_sem.at[i, beside, y])
        for d in (dp, beside, across, corner):
            arrived(wbuf.at[i, d, yo], w_sem.at[i, d, yo])

    relay_z(1)
    relay_x(0)
    relay_z(2)
    relay_w(0)
    relay_z(3)
    relay_x(1)
    relay_w(1)
    relay_x(2)
    relay_x(3)
    columns(0)
    for k in range(1, Z):
        share(0, k)
    columns(1)
    for k in range(1, Z):
        share(1, k)
    copy_a.wait()
    share(0, 0)
    totals = [project(0, 0), project(1, 0)]

    for k in range(Z):
        if k:
            arrived(spbuf.at[line[k] * G + y], s_sem.at[line[k] * G + y])
        arrived(spbuf.at[line[k] * G + yo], s_sem.at[line[k] * G + yo])
    count = Z * G * tokens
    lane = lax.broadcasted_iota(jnp.int32, (1, count), 1)
    key_pos = jnp.zeros((1, count), jnp.int32)
    lanes = spbuf.shape[2]
    for j in range(Z * G):
        for i in range(2):
            base = j * tokens + i * half
            row = spbuf[j, i:i + 1, :]
            row = jnp.concatenate([row] * (count // lanes), axis=1)
            key_pos = jnp.where((lane >= base) & (lane < base + half), row * half + (lane - base), key_pos)
    at = lax.broadcasted_iota(jnp.int32, (tokens, 1), 0)
    own_pos = jnp.where(at < half, span_ref[0] * half + at, span_ref[1] * half + (at - half))
    bias[...] = jnp.where(key_pos <= own_pos, 0.0, -1e30)

    def straight(source, target):
        return (lax.div(2 * source, Z) == lax.div(2 * target, Z)) | (target == 0)

    for i in range(2):
        for k in range(1, Z):
            zs = line[k]
            arrived(got[i].at[zs], p_sem.at[i, zs])
            part = got[i][zs].astype(jnp.float32)
            if i == 0:
                arrived(rgot.at[zs], r_sem.at[zs])
                part *= jnp.sum(jnp.where(diagonal, rgot[zs, 0:1, :], 0.0), axis=1, keepdims=True) * (1.0 / STEPS)
            totals[i] += part
        outs[i][ctx] = totals[i].astype(outs[i].dtype)
        mine, recv = outs[i].at[ctx], g_sem.at[i, ctx]
        for k in range(Z - 1, 0, -1):
            send(mine, mine, recv, dp, line[k] * G + y)
        send(mine, mine, recv, dp, z * G + yo)
        for k in range(Z - 1, 0, -1):
            send_if(straight(z, line[k]), mine, mine, recv, dp, line[k] * G + yo)

    def relay(i):
        for k in range(1, Z):
            src = line[k] * G + y
            slot, recv = outs[i].at[src], g_sem.at[i, src]
            arrived(slot, recv)
            send_if(jnp.logical_not(straight(line[k], z)), slot, slot, recv, dp, z * G + yo)

    def gathered(i):
        for k in range(Z):
            src = line[k] * G + yo
            arrived(outs[i].at[src], g_sem.at[i, src])

    load_q.wait()
    relay(0)
    relay(1)
    gathered(0)
    keys = outs[0][...].reshape(count, hd)
    weights, norms = [], []
    for g in range(q_ref.shape[1]):
        query = q_ref[:, g, :]
        score = lax.dot_general(query, keys, (((1,), (1,)), ((), ())), preferred_element_type=jnp.float32)
        score = score * scale + bias[...]
        weight = jnp.exp(score - jnp.max(score, axis=1, keepdims=True))
        norms.append(jnp.sum(weight, axis=1, keepdims=True))
        weights.append(weight.astype(jnp.bfloat16))
    gathered(1)
    values = outs[1][...].reshape(count, hd)
    for g in range(q_ref.shape[1]):
        mixed = jnp.dot(weights[g], values, preferred_element_type=jnp.float32)
        o_ref[:, g * hd:(g + 1) * hd] = (mixed / norms[g]).astype(o_ref.dtype)

    for copy, want in sent:
        if want is None:
            copy.wait_send()
        else:
            pl.when(want)(copy.wait_send)


def plan(mesh, tokens, shard_rows, heads, head_dim):
    dp, ctx = mesh.shape["dp"], mesh.shape["ctx"]
    if heads != dp or tokens % 16 or tokens > 128 or shard_rows % 16 or head_dim % 128 or (ctx * tokens) % 128:
        return None
    if dp != 4 or ctx != 8 or (2 * shard_rows) % 128:
        return None
    return dp // 2, 2, ctx // 2, 2


def fused(factors, activations, queries, w_kv, span_of):
    X, C, Z, G = factors
    tokens = activations.shape[0]
    shard_rows, heads, _, hd = w_kv.shape
    fw, ctx, dp = G * shard_rows, Z * G, X * C
    group = queries.shape[1]
    dma = pltpu.SemaphoreType.DMA
    bf16, f32 = jnp.bfloat16, jnp.float32
    block = (tokens, hd)
    hbm = pl.BlockSpec(memory_space=pl.ANY)
    sends = 20 * Z + 40
    return pl.pallas_call(
        functools.partial(fused_kernel, X, C, Z, G, 1.0 / math.sqrt(hd)),
        out_shape=pltpu.VMEM((tokens, group * hd), bf16),
        in_specs=[hbm, hbm, hbm, hbm],
        scratch_shapes=[
            pltpu.VMEM(queries.shape, bf16),
            pltpu.VMEM(w_kv.shape, bf16),
            pltpu.VMEM((2, heads, shard_rows, hd), bf16),
            pltpu.VMEM((dp, Z, tokens, fw), bf16),
            pltpu.VMEM((2, dp, G, shard_rows, hd), bf16),
            pltpu.VMEM((Z, *block), jnp.int16),
            pltpu.VMEM((Z, *block), VALUE_PART),
            pltpu.VMEM((Z, *block), jnp.int16),
            pltpu.VMEM((Z, *block), VALUE_PART),
            pltpu.VMEM((Z, 8, 128), f32),
            pltpu.VMEM((Z, 8, 128), f32),
            pltpu.VMEM((ctx, *block), bf16),
            pltpu.VMEM((ctx, *block), bf16),
            pltpu.VMEM((ctx, 8, 128), jnp.int32),
            pltpu.VMEM((tokens, ctx * tokens), f32),
            dma((sends,)), dma((dp, Z)), dma((2, dp, G)), dma((2, Z)), dma((Z,)), dma((2, ctx)), dma((ctx,)), dma((4,)),
            pltpu.SMEM(span_of.shape, jnp.int32),
        ],
        compiler_params=pltpu.CompilerParams(collective_id=0, has_side_effects=True),
        name="fused",
    )(
        activations,
        queries,
        w_kv,
        span_of,
    )


def attend(carry, keys, values, key_pos, query, query_pos, scale):
    top, total, accum = carry
    score = jnp.einsum("tgd,nd->tgn", query, keys, preferred_element_type=jnp.float32) * scale
    visible = (key_pos[None, :] <= query_pos[:, None])[:, None, :]
    new_top = jnp.maximum(top, jnp.max(jnp.where(visible, score, -1e30), axis=2))
    weight = jnp.where(visible, jnp.exp(score - new_top[..., None]), 0.0)
    factor = jnp.exp(top - new_top)
    total = total * factor + jnp.sum(weight, axis=2)
    accum = accum * factor[..., None] + jnp.einsum(
        "tgn,nd->tgd", weight.astype(jnp.bfloat16), values, preferred_element_type=jnp.float32
    )
    return (new_top, total, accum)


def body(activations, queries, w_kv, span_of, mesh=None):
    factors = plan(mesh, activations.shape[0], w_kv.shape[0], w_kv.shape[1], queries.shape[2])
    if factors is not None:
        return fused(factors, activations, queries, w_kv, span_of)
    tokens = activations.shape[0]
    head_dim = queries.shape[2]
    half = tokens // 2
    scale = 1.0 / math.sqrt(head_dim)
    whole = lax.all_gather(activations, "dp", axis=1, tiled=True)
    shard_rows = w_kv.shape[0]
    mine = lax.all_to_all(w_kv, "dp", split_axis=1, concat_axis=0, tiled=True)
    ordered = whole.reshape(tokens, lax.axis_size("dp"), lax.axis_size("ctx"), shard_rows)
    ordered = jnp.transpose(ordered, (0, 2, 1, 3)).reshape(tokens, -1)
    piece = lax.all_gather(mine, "ctx", axis=0, tiled=True)
    count = piece.shape[0]
    projected = jnp.dot(ordered, piece.reshape(count, -1), preferred_element_type=jnp.float32)
    key_value = projected.astype(jnp.bfloat16).reshape(tokens, 2, head_dim)
    all_spans = lax.all_gather(span_of, "ctx", axis=0, tiled=True)
    offsets = jnp.arange(tokens, dtype=jnp.int32)
    own_pos = jnp.where(offsets < half, span_of[0], span_of[1]) * half + offsets % half

    def update(state, part, part_pos):
        return attend(state, part[:, 0], part[:, 1], part_pos, queries, own_pos, scale)

    group = queries.shape[1]
    start_state = (
        jnp.full((tokens, group), -1e30, jnp.float32),
        jnp.zeros((tokens, group), jnp.float32),
        jnp.zeros((tokens, group, head_dim), jnp.float32),
    )
    state = start_state
    piece = lax.all_gather(key_value, "ctx", axis=0, tiled=True)
    count = piece.shape[0]
    index = jnp.arange(count, dtype=jnp.int32)
    key_pos = jnp.take(all_spans, index // half) * half + index % half
    block = 1024 if count % 1024 == 0 else count

    def step(held, item):
        return (update(held, item[0], item[1]), None)

    blocks = (
        piece.reshape(count // block, block, 2, head_dim),
        key_pos.reshape(count // block, block),
    )
    state, _ = lax.scan(step, state, blocks)
    top, total, accum = state
    return (accum / total[..., None]).astype(jnp.bfloat16).reshape(tokens, group * head_dim)


def solution(mesh):
    return jax.shard_map(
        functools.partial(body, mesh=mesh),
        mesh=mesh,
        in_specs=(
            P("ctx", "dp"),
            P("ctx", "dp", None),
            P(("dp", "ctx"), None, None, None),
            P("ctx"),
        ),
        out_specs=P("ctx", "dp"),
        check_vma=False,
    )
```

```python
import functools
import math

import jax
import jax.numpy as jnp
from jax import lax
from jax.experimental import pallas as pl
from jax.experimental.pallas import tpu as pltpu
from jax.sharding import PartitionSpec as P

MESH = pl.DeviceIdType.MESH
VALUE_PART = jnp.bfloat16
STEPS = 32767.0


def remote(src, dst, send, recv, dp, ctx):
    return pltpu.make_async_remote_copy(
        src_ref=src,
        dst_ref=dst,
        send_sem=send,
        recv_sem=recv,
        device_id={"dp": dp, "ctx": ctx},
        device_id_type=MESH,
    )


def fused_kernel(
    X, C, Z, G, scale,
    a_ref, q_in, w_hbm, span_in, o_ref,
    q_ref, w_in, wloc, abuf, wbuf, psum_k, psum_v, got_k, got_v, rsum, rgot, kbuf, vbuf, spbuf, bias,
    send_sem, a_sem, w_sem, p_sem, r_sem, g_sem, s_sem, own_sem, span_ref,
):
    dp, ctx = lax.axis_index("dp"), lax.axis_index("ctx")
    x, c = lax.div(dp, C), lax.rem(dp, C)
    z, y = lax.div(ctx, G), lax.rem(ctx, G)
    tokens = a_ref.shape[0]
    half = tokens // 2
    fw, hd = abuf.shape[3], kbuf.shape[2]
    heads = w_in.shape[1]
    psum, got, outs = (psum_k, psum_v), (got_k, got_v), (kbuf, vbuf)
    xo, co, yo = X - 1 - x, C - 1 - c, G - 1 - y
    across, beside, corner = xo * C + c, x * C + co, xo * C + co

    way = 1 - 2 * lax.div(2 * z, Z)
    edge = (z == 0) | (z == Z - 1)
    line = [z, z + way, jnp.where(edge, z + 2 * way, z - way), jnp.where(edge, z + 3 * way, z + 2 * way)]

    def arrived(slot, recv):
        remote(slot, slot, recv, recv, dp, ctx).wait_recv()

    sent = []

    def send(src, dst, recv, to_dp, to_ctx):
        copy = remote(src, dst, send_sem.at[len(sent)], recv, to_dp, to_ctx)
        sent.append((copy, None))
        copy.start()

    def send_if(want, src, dst, recv, to_dp, to_ctx):
        copy = remote(src, dst, send_sem.at[len(sent)], recv, to_dp, to_ctx)
        sent.append((copy, want))
        pl.when(want)(copy.start)

    peers = [(dp, line[k] * G + y) for k in range(1, Z)]
    peers += [(dp, line[k] * G + yo) for k in range(Z)]
    peers += [(beside, z * G + yo), (across, ctx), (beside, ctx), (corner, ctx)]
    peers += [(across, line[k] * G + y) for k in range(1, Z)]

    def skips(source, target):
        return (jnp.abs(source - target) == Z - 1) | ((jnp.abs(source - target) == 1) & (source + target != Z - 1))

    load_w = pltpu.make_async_copy(w_hbm, w_in, own_sem.at[2])
    load_q = pltpu.make_async_copy(q_in, q_ref, own_sem.at[3])
    barrier = pltpu.get_barrier_semaphore()
    for pd, pc in peers:
        pl.semaphore_signal(barrier, inc=1, device_id={"dp": pd, "ctx": pc}, device_id_type=MESH)
    load_s = pltpu.make_async_copy(span_in, span_ref, own_sem.at[1])
    load_w.start()
    load_s.start()
    own_a = a_ref.at[:, pl.ds(pl.multiple_of(z * fw, fw), fw)]
    copy_a = pltpu.make_async_copy(own_a, abuf.at[dp, z], own_sem.at[0])
    copy_a.start()
    load_q.start()
    pl.semaphore_wait(barrier, len(peers))

    for k in range(1, Z):
        zt = line[k]
        send(a_ref.at[:, pl.ds(pl.multiple_of(zt * fw, fw), fw)], abuf.at[dp, z],
             a_sem.at[dp, z], dp, zt * G + y)
    for k in range(1, Z):
        send_if(skips(z, line[k]), a_ref.at[:, pl.ds(pl.multiple_of(line[k] * fw, fw), fw)], abuf.at[dp, z],
                a_sem.at[dp, z], across, line[k] * G + y)
    send(own_a, abuf.at[dp, z], a_sem.at[dp, z], across, ctx)
    send(own_a, abuf.at[dp, z], a_sem.at[dp, z], beside, ctx)
    load_w.wait()
    for i in range(2):
        for h in range(heads):
            wloc[i, h] = w_in[:, h, i, :]
        slot, recv = wbuf.at[i, dp, y], w_sem.at[i, dp, y]
        for h in (across, corner):
            send(wloc.at[i, h], slot, recv, h, ctx)
        for h in (dp, beside):
            send(wloc.at[i, h], slot, recv, h, z * G + yo)
        send(wloc.at[i, beside], slot, recv, beside, ctx)
        wbuf[i, dp, y] = wloc[i, dp]
    load_s.wait()
    spbuf[ctx] = jnp.where(
        lax.broadcasted_iota(jnp.int32, spbuf.shape[1:], 0) == 0, span_ref[0], span_ref[1]
    )
    for k in range(Z):
        if k:
            send(spbuf.at[ctx], spbuf.at[ctx], s_sem.at[ctx], dp, line[k] * G + y)
        send(spbuf.at[ctx], spbuf.at[ctx], s_sem.at[ctx], dp, line[k] * G + yo)

    def relay_w(i):
        for d in (across, corner):
            slot, recv = wbuf.at[i, d, y], w_sem.at[i, d, y]
            arrived(slot, recv)
            send(slot, slot, recv, dp, z * G + yo)

    def relay_z(k):
        slot, recv = abuf.at[dp, line[k]], a_sem.at[dp, line[k]]
        arrived(slot, recv)
        send_if(jnp.logical_not(skips(line[k], z)), slot, slot, recv, across, ctx)
        send(slot, slot, recv, beside, ctx)

    def relay_x(k):
        slot, recv = abuf.at[across, line[k]], a_sem.at[across, line[k]]
        arrived(slot, recv)
        send(slot, slot, recv, beside, ctx)

    lanes = rsum.shape[2]
    diagonal = lax.broadcasted_iota(jnp.int32, (tokens, lanes), 0) == lax.broadcasted_iota(jnp.int32, (tokens, lanes), 1)

    def project(i, k):
        rows = [abuf[d, line[k]] for d in range(X * C)]
        held = None
        for d in range(X * C):
            part = jnp.dot(rows[d], wbuf[i, d].reshape(fw, hd), preferred_element_type=jnp.float32)
            held = part if held is None else held + part
        return held

    def share(i, k):
        if i == 0:
            for d in (beside, corner):
                arrived(abuf.at[d, line[k]], a_sem.at[d, line[k]])
        if k:
            part = project(i, k)
            if i == 0:
                peak = jnp.maximum(jnp.max(jnp.abs(part), axis=1, keepdims=True), 1e-30)
                part = jnp.round(part * (STEPS / peak)).astype(jnp.int32)
                peaks = jnp.sum(jnp.where(diagonal, peak, 0.0), axis=0, keepdims=True)
                rsum[line[k]] = jnp.broadcast_to(peaks, rsum.shape[1:])
                send(rsum.at[line[k]], rgot.at[z], r_sem.at[z], dp, line[k] * G + y)
            psum[i][line[k]] = part.astype(psum[i].dtype)
            send(psum[i].at[line[k]], got[i].at[z], p_sem.at[i, z], dp, line[k] * G + y)

    def columns(i):
        arrived(wbuf.at[i, beside, y], w_sem.at[i, beside, y])
        for d in (dp, beside, across, corner):
            arrived(wbuf.at[i, d, yo], w_sem.at[i, d, yo])

    relay_z(1)
    relay_x(0)
    relay_z(2)
    relay_w(0)
    relay_z(3)
    relay_x(1)
    relay_w(1)
    relay_x(2)
    relay_x(3)
    columns(0)
    for k in range(1, Z):
        share(0, k)
    columns(1)
    for k in range(1, Z):
        share(1, k)
    copy_a.wait()
    share(0, 0)
    totals = [project(0, 0), project(1, 0)]

    for k in range(Z):
        if k:
            arrived(spbuf.at[line[k] * G + y], s_sem.at[line[k] * G + y])
        arrived(spbuf.at[line[k] * G + yo], s_sem.at[line[k] * G + yo])
    count = Z * G * tokens
    lane = lax.broadcasted_iota(jnp.int32, (1, count), 1)
    key_pos = jnp.zeros((1, count), jnp.int32)
    lanes = spbuf.shape[2]
    for j in range(Z * G):
        for i in range(2):
            base = j * tokens + i * half
            row = spbuf[j, i:i + 1, :]
            row = jnp.concatenate([row] * (count // lanes), axis=1)
            key_pos = jnp.where((lane >= base) & (lane < base + half), row * half + (lane - base), key_pos)
    at = lax.broadcasted_iota(jnp.int32, (tokens, 1), 0)
    own_pos = jnp.where(at < half, span_ref[0] * half + at, span_ref[1] * half + (at - half))
    bias[...] = jnp.where(key_pos <= own_pos, 0.0, -1e30)

    def straight(source, target):
        return (lax.div(2 * source, Z) == lax.div(2 * target, Z)) | ((target == 0) & (c == 0))

    for i in range(2):
        for k in range(1, Z):
            zs = line[k]
            arrived(got[i].at[zs], p_sem.at[i, zs])
            part = got[i][zs].astype(jnp.float32)
            if i == 0:
                arrived(rgot.at[zs], r_sem.at[zs])
                part *= jnp.sum(jnp.where(diagonal, rgot[zs, 0:1, :], 0.0), axis=1, keepdims=True) * (1.0 / STEPS)
            totals[i] += part
        outs[i][ctx] = totals[i].astype(outs[i].dtype)
        mine, recv = outs[i].at[ctx], g_sem.at[i, ctx]
        for k in range(1, Z):
            send(mine, mine, recv, dp, line[k] * G + y)
        send(mine, mine, recv, dp, z * G + yo)
        for k in range(1, Z):
            send_if(straight(z, line[k]), mine, mine, recv, dp, line[k] * G + yo)

    def relay(i):
        for k in range(1, Z):
            src = line[k] * G + y
            slot, recv = outs[i].at[src], g_sem.at[i, src]
            arrived(slot, recv)
            send_if(jnp.logical_not(straight(line[k], z)), slot, slot, recv, dp, z * G + yo)

    def gathered(i):
        for k in range(Z):
            src = line[k] * G + yo
            arrived(outs[i].at[src], g_sem.at[i, src])

    load_q.wait()
    relay(0)
    relay(1)
    gathered(0)
    keys = outs[0][...].reshape(count, hd)
    weights, norms = [], []
    for g in range(q_ref.shape[1]):
        query = q_ref[:, g, :]
        score = lax.dot_general(query, keys, (((1,), (1,)), ((), ())), preferred_element_type=jnp.float32)
        score = score * scale + bias[...]
        weight = jnp.exp(score - jnp.max(score, axis=1, keepdims=True))
        norms.append(jnp.sum(weight, axis=1, keepdims=True))
        weights.append(weight.astype(jnp.bfloat16))
    gathered(1)
    values = outs[1][...].reshape(count, hd)
    for g in range(q_ref.shape[1]):
        mixed = jnp.dot(weights[g], values, preferred_element_type=jnp.float32)
        o_ref[:, g * hd:(g + 1) * hd] = (mixed / norms[g]).astype(o_ref.dtype)

    for copy, want in sent:
        if want is None:
            copy.wait_send()
        else:
            pl.when(want)(copy.wait_send)


def plan(mesh, tokens, shard_rows, heads, head_dim):
    dp, ctx = mesh.shape["dp"], mesh.shape["ctx"]
    if heads != dp or tokens % 16 or tokens > 128 or shard_rows % 16 or head_dim % 128 or (ctx * tokens) % 128:
        return None
    if dp != 4 or ctx != 8 or (2 * shard_rows) % 128:
        return None
    return dp // 2, 2, ctx // 2, 2


def fused(factors, activations, queries, w_kv, span_of):
    X, C, Z, G = factors
    tokens = activations.shape[0]
    shard_rows, heads, _, hd = w_kv.shape
    fw, ctx, dp = G * shard_rows, Z * G, X * C
    group = queries.shape[1]
    dma = pltpu.SemaphoreType.DMA
    bf16, f32 = jnp.bfloat16, jnp.float32
    block = (tokens, hd)
    hbm = pl.BlockSpec(memory_space=pl.ANY)
    sends = 20 * Z + 40
    return pl.pallas_call(
        functools.partial(fused_kernel, X, C, Z, G, 1.0 / math.sqrt(hd)),
        out_shape=pltpu.VMEM((tokens, group * hd), bf16),
        in_specs=[hbm, hbm, hbm, hbm],
        scratch_shapes=[
            pltpu.VMEM(queries.shape, bf16),
            pltpu.VMEM(w_kv.shape, bf16),
            pltpu.VMEM((2, heads, shard_rows, hd), bf16),
            pltpu.VMEM((dp, Z, tokens, fw), bf16),
            pltpu.VMEM((2, dp, G, shard_rows, hd), bf16),
            pltpu.VMEM((Z, *block), jnp.int16),
            pltpu.VMEM((Z, *block), VALUE_PART),
            pltpu.VMEM((Z, *block), jnp.int16),
            pltpu.VMEM((Z, *block), VALUE_PART),
            pltpu.VMEM((Z, 8, 128), f32),
            pltpu.VMEM((Z, 8, 128), f32),
            pltpu.VMEM((ctx, *block), bf16),
            pltpu.VMEM((ctx, *block), bf16),
            pltpu.VMEM((ctx, 8, 128), jnp.int32),
            pltpu.VMEM((tokens, ctx * tokens), f32),
            dma((sends,)), dma((dp, Z)), dma((2, dp, G)), dma((2, Z)), dma((Z,)), dma((2, ctx)), dma((ctx,)), dma((4,)),
            pltpu.SMEM(span_of.shape, jnp.int32),
        ],
        compiler_params=pltpu.CompilerParams(collective_id=0, has_side_effects=True),
        name="fused",
    )(
        activations,
        queries,
        w_kv,
        span_of,
    )


def attend(carry, keys, values, key_pos, query, query_pos, scale):
    top, total, accum = carry
    score = jnp.einsum("tgd,nd->tgn", query, keys, preferred_element_type=jnp.float32) * scale
    visible = (key_pos[None, :] <= query_pos[:, None])[:, None, :]
    new_top = jnp.maximum(top, jnp.max(jnp.where(visible, score, -1e30), axis=2))
    weight = jnp.where(visible, jnp.exp(score - new_top[..., None]), 0.0)
    factor = jnp.exp(top - new_top)
    total = total * factor + jnp.sum(weight, axis=2)
    accum = accum * factor[..., None] + jnp.einsum(
        "tgn,nd->tgd", weight.astype(jnp.bfloat16), values, preferred_element_type=jnp.float32
    )
    return (new_top, total, accum)


def body(activations, queries, w_kv, span_of, mesh=None):
    factors = plan(mesh, activations.shape[0], w_kv.shape[0], w_kv.shape[1], queries.shape[2])
    if factors is not None:
        return fused(factors, activations, queries, w_kv, span_of)
    tokens = activations.shape[0]
    head_dim = queries.shape[2]
    half = tokens // 2
    scale = 1.0 / math.sqrt(head_dim)
    whole = lax.all_gather(activations, "dp", axis=1, tiled=True)
    shard_rows = w_kv.shape[0]
    mine = lax.all_to_all(w_kv, "dp", split_axis=1, concat_axis=0, tiled=True)
    ordered = whole.reshape(tokens, lax.axis_size("dp"), lax.axis_size("ctx"), shard_rows)
    ordered = jnp.transpose(ordered, (0, 2, 1, 3)).reshape(tokens, -1)
    piece = lax.all_gather(mine, "ctx", axis=0, tiled=True)
    count = piece.shape[0]
    projected = jnp.dot(ordered, piece.reshape(count, -1), preferred_element_type=jnp.float32)
    key_value = projected.astype(jnp.bfloat16).reshape(tokens, 2, head_dim)
    all_spans = lax.all_gather(span_of, "ctx", axis=0, tiled=True)
    offsets = jnp.arange(tokens, dtype=jnp.int32)
    own_pos = jnp.where(offsets < half, span_of[0], span_of[1]) * half + offsets % half

    def update(state, part, part_pos):
        return attend(state, part[:, 0], part[:, 1], part_pos, queries, own_pos, scale)

    group = queries.shape[1]
    start_state = (
        jnp.full((tokens, group), -1e30, jnp.float32),
        jnp.zeros((tokens, group), jnp.float32),
        jnp.zeros((tokens, group, head_dim), jnp.float32),
    )
    state = start_state
    piece = lax.all_gather(key_value, "ctx", axis=0, tiled=True)
    count = piece.shape[0]
    index = jnp.arange(count, dtype=jnp.int32)
    key_pos = jnp.take(all_spans, index // half) * half + index % half
    block = 1024 if count % 1024 == 0 else count

    def step(held, item):
        return (update(held, item[0], item[1]), None)

    blocks = (
        piece.reshape(count // block, block, 2, head_dim),
        key_pos.reshape(count // block, block),
    )
    state, _ = lax.scan(step, state, blocks)
    top, total, accum = state
    return (accum / total[..., None]).astype(jnp.bfloat16).reshape(tokens, group * head_dim)


def solution(mesh):
    return jax.shard_map(
        functools.partial(body, mesh=mesh),
        mesh=mesh,
        in_specs=(
            P("ctx", "dp"),
            P("ctx", "dp", None),
            P(("dp", "ctx"), None, None, None),
            P("ctx"),
        ),
        out_specs=P("ctx", "dp"),
        check_vma=False,
    )
```

```python
import functools
import math

import jax
import jax.numpy as jnp
from jax import lax
from jax.experimental import pallas as pl
from jax.experimental.pallas import tpu as pltpu
from jax.sharding import PartitionSpec as P

MESH = pl.DeviceIdType.MESH
VALUE_PART = jnp.bfloat16
STEPS = 32767.0


def remote(src, dst, send, recv, dp, ctx):
    return pltpu.make_async_remote_copy(
        src_ref=src,
        dst_ref=dst,
        send_sem=send,
        recv_sem=recv,
        device_id={"dp": dp, "ctx": ctx},
        device_id_type=MESH,
    )


def fused_kernel(
    X, C, Z, G, scale,
    a_hbm, q_in, w_hbm, span_in, o_ref,
    q_ref, w_in, wloc, abuf, wbuf, psum_k, psum_v, got_k, got_v, rsum, rgot, kbuf, vbuf, spbuf, bias,
    send_sem, a_sem, w_sem, p_sem, r_sem, g_sem, s_sem, own_sem, span_ref, a_ref,
):
    dp, ctx = lax.axis_index("dp"), lax.axis_index("ctx")
    x, c = lax.div(dp, C), lax.rem(dp, C)
    z, y = lax.div(ctx, G), lax.rem(ctx, G)
    tokens = a_ref.shape[0]
    half = tokens // 2
    fw, hd = abuf.shape[3], kbuf.shape[2]
    heads = w_in.shape[1]
    psum, got, outs = (psum_k, psum_v), (got_k, got_v), (kbuf, vbuf)
    xo, co, yo = X - 1 - x, C - 1 - c, G - 1 - y
    across, beside, corner = xo * C + c, x * C + co, xo * C + co

    way = 1 - 2 * lax.div(2 * z, Z)
    edge = (z == 0) | (z == Z - 1)
    line = [z, z + way, jnp.where(edge, z + 2 * way, z - way), jnp.where(edge, z + 3 * way, z + 2 * way)]

    def arrived(slot, recv):
        remote(slot, slot, recv, recv, dp, ctx).wait_recv()

    sent = []

    def send(src, dst, recv, to_dp, to_ctx):
        copy = remote(src, dst, send_sem.at[len(sent)], recv, to_dp, to_ctx)
        sent.append((copy, None))
        copy.start()

    def send_if(want, src, dst, recv, to_dp, to_ctx):
        copy = remote(src, dst, send_sem.at[len(sent)], recv, to_dp, to_ctx)
        sent.append((copy, want))
        pl.when(want)(copy.start)

    peers = [(dp, line[k] * G + y) for k in range(1, Z)]
    peers += [(dp, line[k] * G + yo) for k in range(Z)]
    peers += [(beside, z * G + yo), (across, ctx), (beside, ctx), (corner, ctx)]
    peers += [(across, line[k] * G + y) for k in range(1, Z)]

    def skips(source, target):
        return (jnp.abs(source - target) == Z - 1) | ((jnp.abs(source - target) == 1) & (source + target != Z - 1))

    load_w = pltpu.make_async_copy(w_hbm, w_in, own_sem.at[2])
    load_q = pltpu.make_async_copy(q_in, q_ref, own_sem.at[3])
    load_a = pltpu.make_async_copy(a_hbm, a_ref, own_sem.at[4])
    barrier = pltpu.get_barrier_semaphore()
    for pd, pc in peers:
        pl.semaphore_signal(barrier, inc=1, device_id={"dp": pd, "ctx": pc}, device_id_type=MESH)
    load_s = pltpu.make_async_copy(span_in, span_ref, own_sem.at[1])
    load_a.start()
    load_w.start()
    load_s.start()
    own_a = a_ref.at[:, pl.ds(pl.multiple_of(z * fw, fw), fw)]
    copy_a = pltpu.make_async_copy(own_a, abuf.at[dp, z], own_sem.at[0])
    load_q.start()
    pl.semaphore_wait(barrier, len(peers))
    load_a.wait()
    copy_a.start()

    for k in range(1, Z):
        zt = line[k]
        send(a_ref.at[:, pl.ds(pl.multiple_of(zt * fw, fw), fw)], abuf.at[dp, z],
             a_sem.at[dp, z], dp, zt * G + y)
    for k in range(1, Z):
        send_if(skips(z, line[k]), a_ref.at[:, pl.ds(pl.multiple_of(line[k] * fw, fw), fw)], abuf.at[dp, z],
                a_sem.at[dp, z], across, line[k] * G + y)
    send(own_a, abuf.at[dp, z], a_sem.at[dp, z], across, ctx)
    send(own_a, abuf.at[dp, z], a_sem.at[dp, z], beside, ctx)
    load_w.wait()
    for i in range(2):
        for h in range(heads):
            wloc[i, h] = w_in[:, h, i, :]
        slot, recv = wbuf.at[i, dp, y], w_sem.at[i, dp, y]
        for h in (across, corner):
            send(wloc.at[i, h], slot, recv, h, ctx)
        for h in (dp, beside):
            send(wloc.at[i, h], slot, recv, h, z * G + yo)
        send(wloc.at[i, beside], slot, recv, beside, ctx)
        wbuf[i, dp, y] = wloc[i, dp]
    load_s.wait()
    spbuf[ctx] = jnp.where(
        lax.broadcasted_iota(jnp.int32, spbuf.shape[1:], 0) == 0, span_ref[0], span_ref[1]
    )
    for k in range(Z):
        if k:
            send(spbuf.at[ctx], spbuf.at[ctx], s_sem.at[ctx], dp, line[k] * G + y)
        send(spbuf.at[ctx], spbuf.at[ctx], s_sem.at[ctx], dp, line[k] * G + yo)

    def relay_w(i):
        for d in (across, corner):
            slot, recv = wbuf.at[i, d, y], w_sem.at[i, d, y]
            arrived(slot, recv)
            send(slot, slot, recv, dp, z * G + yo)

    def relay_z(k):
        slot, recv = abuf.at[dp, line[k]], a_sem.at[dp, line[k]]
        arrived(slot, recv)
        send_if(jnp.logical_not(skips(line[k], z)), slot, slot, recv, across, ctx)
        send(slot, slot, recv, beside, ctx)

    def relay_x(k):
        slot, recv = abuf.at[across, line[k]], a_sem.at[across, line[k]]
        arrived(slot, recv)
        send(slot, slot, recv, beside, ctx)

    lanes = rsum.shape[2]
    diagonal = lax.broadcasted_iota(jnp.int32, (tokens, lanes), 0) == lax.broadcasted_iota(jnp.int32, (tokens, lanes), 1)

    def project(i, k):
        rows = [abuf[d, line[k]] for d in range(X * C)]
        held = None
        for d in range(X * C):
            part = jnp.dot(rows[d], wbuf[i, d].reshape(fw, hd), preferred_element_type=jnp.float32)
            held = part if held is None else held + part
        return held

    def share(i, k):
        if i == 0:
            for d in (beside, corner):
                arrived(abuf.at[d, line[k]], a_sem.at[d, line[k]])
        if k:
            part = project(i, k)
            if i == 0:
                peak = jnp.maximum(jnp.max(jnp.abs(part), axis=1, keepdims=True), 1e-30)
                part = jnp.round(part * (STEPS / peak)).astype(jnp.int32)
                peaks = jnp.sum(jnp.where(diagonal, peak, 0.0), axis=0, keepdims=True)
                rsum[line[k]] = jnp.broadcast_to(peaks, rsum.shape[1:])
                send(rsum.at[line[k]], rgot.at[z], r_sem.at[z], dp, line[k] * G + y)
            psum[i][line[k]] = part.astype(psum[i].dtype)
            send(psum[i].at[line[k]], got[i].at[z], p_sem.at[i, z], dp, line[k] * G + y)

    def columns(i):
        arrived(wbuf.at[i, beside, y], w_sem.at[i, beside, y])
        for d in (dp, beside, across, corner):
            arrived(wbuf.at[i, d, yo], w_sem.at[i, d, yo])

    relay_z(1)
    relay_x(0)
    relay_z(2)
    relay_w(0)
    relay_z(3)
    relay_x(1)
    relay_w(1)
    relay_x(2)
    relay_x(3)
    columns(0)
    for k in range(1, Z):
        share(0, k)
    columns(1)
    for k in range(1, Z):
        share(1, k)
    copy_a.wait()
    share(0, 0)
    totals = [project(0, 0), project(1, 0)]

    for k in range(Z):
        if k:
            arrived(spbuf.at[line[k] * G + y], s_sem.at[line[k] * G + y])
        arrived(spbuf.at[line[k] * G + yo], s_sem.at[line[k] * G + yo])
    count = Z * G * tokens
    lane = lax.broadcasted_iota(jnp.int32, (1, count), 1)
    key_pos = jnp.zeros((1, count), jnp.int32)
    lanes = spbuf.shape[2]
    for j in range(Z * G):
        for i in range(2):
            base = j * tokens + i * half
            row = spbuf[j, i:i + 1, :]
            row = jnp.concatenate([row] * (count // lanes), axis=1)
            key_pos = jnp.where((lane >= base) & (lane < base + half), row * half + (lane - base), key_pos)
    at = lax.broadcasted_iota(jnp.int32, (tokens, 1), 0)
    own_pos = jnp.where(at < half, span_ref[0] * half + at, span_ref[1] * half + (at - half))
    bias[...] = jnp.where(key_pos <= own_pos, 0.0, -1e30)

    def straight(source, target):
        return (lax.div(2 * source, Z) == lax.div(2 * target, Z)) | ((target == 0) & (c == 0))

    for i in range(2):
        for k in range(1, Z):
            zs = line[k]
            arrived(got[i].at[zs], p_sem.at[i, zs])
            part = got[i][zs].astype(jnp.float32)
            if i == 0:
                arrived(rgot.at[zs], r_sem.at[zs])
                part *= jnp.sum(jnp.where(diagonal, rgot[zs, 0:1, :], 0.0), axis=1, keepdims=True) * (1.0 / STEPS)
            totals[i] += part
        outs[i][ctx] = totals[i].astype(outs[i].dtype)
        mine, recv = outs[i].at[ctx], g_sem.at[i, ctx]
        for k in (3, 1, 2):
            send(mine, mine, recv, dp, line[k] * G + y)
        send_if(straight(z, line[3]), mine, mine, recv, dp, line[3] * G + yo)
        send(mine, mine, recv, dp, z * G + yo)
        for k in (1, 2):
            send_if(straight(z, line[k]), mine, mine, recv, dp, line[k] * G + yo)

    def relay(i):
        for k in range(1, Z):
            src = line[k] * G + y
            slot, recv = outs[i].at[src], g_sem.at[i, src]
            arrived(slot, recv)
            send_if(jnp.logical_not(straight(line[k], z)), slot, slot, recv, dp, z * G + yo)

    def gathered(i):
        for k in range(Z):
            src = line[k] * G + yo
            arrived(outs[i].at[src], g_sem.at[i, src])

    load_q.wait()
    relay(0)
    relay(1)
    gathered(0)
    keys = outs[0][...].reshape(count, hd)
    weights, norms = [], []
    for g in range(q_ref.shape[1]):
        query = q_ref[:, g, :]
        score = lax.dot_general(query, keys, (((1,), (1,)), ((), ())), preferred_element_type=jnp.float32)
        score = score * scale + bias[...]
        weight = jnp.exp(score - jnp.max(score, axis=1, keepdims=True))
        norms.append(jnp.sum(weight, axis=1, keepdims=True))
        weights.append(weight.astype(jnp.bfloat16))
    gathered(1)
    values = outs[1][...].reshape(count, hd)
    for g in range(q_ref.shape[1]):
        mixed = jnp.dot(weights[g], values, preferred_element_type=jnp.float32)
        o_ref[:, g * hd:(g + 1) * hd] = (mixed / norms[g]).astype(o_ref.dtype)

    for copy, want in sent:
        if want is None:
            copy.wait_send()
        else:
            pl.when(want)(copy.wait_send)


def plan(mesh, tokens, shard_rows, heads, head_dim):
    dp, ctx = mesh.shape["dp"], mesh.shape["ctx"]
    if heads != dp or tokens % 16 or tokens > 128 or shard_rows % 16 or head_dim % 128 or (ctx * tokens) % 128:
        return None
    if dp != 4 or ctx != 8 or (2 * shard_rows) % 128:
        return None
    return dp // 2, 2, ctx // 2, 2


def fused(factors, activations, queries, w_kv, span_of):
    X, C, Z, G = factors
    tokens = activations.shape[0]
    shard_rows, heads, _, hd = w_kv.shape
    fw, ctx, dp = G * shard_rows, Z * G, X * C
    group = queries.shape[1]
    dma = pltpu.SemaphoreType.DMA
    bf16, f32 = jnp.bfloat16, jnp.float32
    block = (tokens, hd)
    hbm = pl.BlockSpec(memory_space=pl.ANY)
    sends = 20 * Z + 40
    return pl.pallas_call(
        functools.partial(fused_kernel, X, C, Z, G, 1.0 / math.sqrt(hd)),
        out_shape=pltpu.VMEM((tokens, group * hd), bf16),
        in_specs=[hbm, hbm, hbm, hbm],
        scratch_shapes=[
            pltpu.VMEM(queries.shape, bf16),
            pltpu.VMEM(w_kv.shape, bf16),
            pltpu.VMEM((2, heads, shard_rows, hd), bf16),
            pltpu.VMEM((dp, Z, tokens, fw), bf16),
            pltpu.VMEM((2, dp, G, shard_rows, hd), bf16),
            pltpu.VMEM((Z, *block), jnp.int16),
            pltpu.VMEM((Z, *block), VALUE_PART),
            pltpu.VMEM((Z, *block), jnp.int16),
            pltpu.VMEM((Z, *block), VALUE_PART),
            pltpu.VMEM((Z, 8, 128), f32),
            pltpu.VMEM((Z, 8, 128), f32),
            pltpu.VMEM((ctx, *block), bf16),
            pltpu.VMEM((ctx, *block), bf16),
            pltpu.VMEM((ctx, 8, 128), jnp.int32),
            pltpu.VMEM((tokens, ctx * tokens), f32),
            dma((sends,)), dma((dp, Z)), dma((2, dp, G)), dma((2, Z)), dma((Z,)), dma((2, ctx)), dma((ctx,)), dma((5,)),
            pltpu.SMEM(span_of.shape, jnp.int32),
            pltpu.VMEM(activations.shape, bf16),
        ],
        compiler_params=pltpu.CompilerParams(collective_id=0, has_side_effects=True),
        name="fused",
    )(
        activations,
        queries,
        w_kv,
        span_of,
    )


def attend(carry, keys, values, key_pos, query, query_pos, scale):
    top, total, accum = carry
    score = jnp.einsum("tgd,nd->tgn", query, keys, preferred_element_type=jnp.float32) * scale
    visible = (key_pos[None, :] <= query_pos[:, None])[:, None, :]
    new_top = jnp.maximum(top, jnp.max(jnp.where(visible, score, -1e30), axis=2))
    weight = jnp.where(visible, jnp.exp(score - new_top[..., None]), 0.0)
    factor = jnp.exp(top - new_top)
    total = total * factor + jnp.sum(weight, axis=2)
    accum = accum * factor[..., None] + jnp.einsum(
        "tgn,nd->tgd", weight.astype(jnp.bfloat16), values, preferred_element_type=jnp.float32
    )
    return (new_top, total, accum)


def body(activations, queries, w_kv, span_of, mesh=None):
    factors = plan(mesh, activations.shape[0], w_kv.shape[0], w_kv.shape[1], queries.shape[2])
    if factors is not None:
        return fused(factors, activations, queries, w_kv, span_of)
    tokens = activations.shape[0]
    head_dim = queries.shape[2]
    half = tokens // 2
    scale = 1.0 / math.sqrt(head_dim)
    whole = lax.all_gather(activations, "dp", axis=1, tiled=True)
    shard_rows = w_kv.shape[0]
    mine = lax.all_to_all(w_kv, "dp", split_axis=1, concat_axis=0, tiled=True)
    ordered = whole.reshape(tokens, lax.axis_size("dp"), lax.axis_size("ctx"), shard_rows)
    ordered = jnp.transpose(ordered, (0, 2, 1, 3)).reshape(tokens, -1)
    piece = lax.all_gather(mine, "ctx", axis=0, tiled=True)
    count = piece.shape[0]
    projected = jnp.dot(ordered, piece.reshape(count, -1), preferred_element_type=jnp.float32)
    key_value = projected.astype(jnp.bfloat16).reshape(tokens, 2, head_dim)
    all_spans = lax.all_gather(span_of, "ctx", axis=0, tiled=True)
    offsets = jnp.arange(tokens, dtype=jnp.int32)
    own_pos = jnp.where(offsets < half, span_of[0], span_of[1]) * half + offsets % half

    def update(state, part, part_pos):
        return attend(state, part[:, 0], part[:, 1], part_pos, queries, own_pos, scale)

    group = queries.shape[1]
    start_state = (
        jnp.full((tokens, group), -1e30, jnp.float32),
        jnp.zeros((tokens, group), jnp.float32),
        jnp.zeros((tokens, group, head_dim), jnp.float32),
    )
    state = start_state
    piece = lax.all_gather(key_value, "ctx", axis=0, tiled=True)
    count = piece.shape[0]
    index = jnp.arange(count, dtype=jnp.int32)
    key_pos = jnp.take(all_spans, index // half) * half + index % half
    block = 1024 if count % 1024 == 0 else count

    def step(held, item):
        return (update(held, item[0], item[1]), None)

    blocks = (
        piece.reshape(count // block, block, 2, head_dim),
        key_pos.reshape(count // block, block),
    )
    state, _ = lax.scan(step, state, blocks)
    top, total, accum = state
    return (accum / total[..., None]).astype(jnp.bfloat16).reshape(tokens, group * head_dim)


def solution(mesh):
    return jax.shard_map(
        functools.partial(body, mesh=mesh),
        mesh=mesh,
        in_specs=(
            P("ctx", "dp"),
            P("ctx", "dp", None),
            P(("dp", "ctx"), None, None, None),
            P("ctx"),
        ),
        out_specs=P("ctx", "dp"),
        check_vma=False,
    )
```

```python
import functools
import math

import jax
import jax.numpy as jnp
from jax import lax
from jax.experimental import pallas as pl
from jax.experimental.pallas import tpu as pltpu
from jax.sharding import PartitionSpec as P

MESH = pl.DeviceIdType.MESH
VALUE_PART = jnp.bfloat16
STEPS = 32767.0
ORDERS = ((('z', 1), ('x', 1), ('x', 0), ('z', 2), ('w', 0), ('z', 3), ('w', 1), ('x', 3), ('x', 2)), (('z', 1), ('x', 0), ('w', 0), ('z', 3), ('z', 2), ('x', 1), ('w', 1), ('x', 2), ('x', 3)), (('z', 2), ('z', 1), ('x', 0), ('w', 0), ('z', 3), ('x', 1), ('w', 1), ('x', 2), ('x', 3)), (('z', 1), ('x', 0), ('z', 2), ('w', 0), ('z', 3), ('x', 1), ('w', 1), ('x', 2), ('x', 3)))
FIRST = (('line', 1), ('line', 2), ('line', 3), ('both', 1), ('both', 2), ('core', 0), ('both', 3), ('x', 0))
GATHER = (('line', 3), ('over', 3), ('line', 2), ('line', 1), ('over', 0), ('over', 2), ('over', 1))
KEYS = (1, 2, 3)
VALUES = (1, 2, 3)


def remote(src, dst, send, recv, dp, ctx):
    return pltpu.make_async_remote_copy(
        src_ref=src,
        dst_ref=dst,
        send_sem=send,
        recv_sem=recv,
        device_id={"dp": dp, "ctx": ctx},
        device_id_type=MESH,
    )


def fused_kernel(
    X, C, Z, G, scale,
    a_hbm, q_in, w_hbm, span_in, o_ref,
    q_ref, w_in, wloc, abuf, wbuf, psum_k, psum_v, got_k, got_v, rsum, rgot, kbuf, vbuf, spbuf, bias,
    send_sem, a_sem, w_sem, p_sem, r_sem, g_sem, s_sem, own_sem, span_ref, a_ref,
):
    dp, ctx = lax.axis_index("dp"), lax.axis_index("ctx")
    x, c = lax.div(dp, C), lax.rem(dp, C)
    z, y = lax.div(ctx, G), lax.rem(ctx, G)
    tokens = a_ref.shape[0]
    half = tokens // 2
    fw, hd = abuf.shape[3], kbuf.shape[2]
    heads = w_in.shape[1]
    psum, got, outs = (psum_k, psum_v), (got_k, got_v), (kbuf, vbuf)
    xo, co, yo = X - 1 - x, C - 1 - c, G - 1 - y
    across, beside, corner = xo * C + c, x * C + co, xo * C + co

    way = 1 - 2 * lax.div(2 * z, Z)
    edge = (z == 0) | (z == Z - 1)
    line = [z, z + way, jnp.where(edge, z + 2 * way, z - way), jnp.where(edge, z + 3 * way, z + 2 * way)]

    def arrived(slot, recv):
        remote(slot, slot, recv, recv, dp, ctx).wait_recv()

    sent = {}

    def send(src, dst, recv, to_dp, to_ctx, want=None, name=None):
        key = len(sent) if name is None else name
        n = sent.setdefault(key, (len(sent), want, (tuple(src.shape), jnp.dtype(src.dtype))))[0]
        copy = remote(src, dst, send_sem.at[n], recv, to_dp, to_ctx)
        if want is None:
            copy.start()
        else:
            pl.when(want)(copy.start)

    def send_if(want, *args, **kwargs):
        send(*args, want=want, **kwargs)

    peers = [(dp, line[k] * G + y) for k in range(1, Z)]
    peers += [(dp, line[k] * G + yo) for k in range(Z)]
    peers += [(beside, z * G + yo), (across, ctx), (beside, ctx), (corner, ctx)]
    peers += [(across, line[k] * G + y) for k in range(1, Z)]

    def skips(source, target):
        return (jnp.abs(source - target) == Z - 1) | ((jnp.abs(source - target) == 1) & (source + target != Z - 1))

    load_w = pltpu.make_async_copy(w_hbm, w_in, own_sem.at[2])
    load_q = pltpu.make_async_copy(q_in, q_ref, own_sem.at[3])
    load_a = pltpu.make_async_copy(a_hbm, a_ref, own_sem.at[4])
    barrier = pltpu.get_barrier_semaphore()
    for pd, pc in peers:
        pl.semaphore_signal(barrier, inc=1, device_id={"dp": pd, "ctx": pc}, device_id_type=MESH)
    load_s = pltpu.make_async_copy(span_in, span_ref, own_sem.at[1])
    load_a.start()
    load_w.start()
    load_s.start()
    own_a = a_ref.at[:, pl.ds(pl.multiple_of(z * fw, fw), fw)]
    copy_a = pltpu.make_async_copy(own_a, abuf.at[dp, z], own_sem.at[0])
    load_q.start()
    pl.semaphore_wait(barrier, len(peers))
    load_a.wait()
    copy_a.start()

    for kind, k in FIRST:
        piece = a_ref.at[:, pl.ds(pl.multiple_of(line[k] * fw, fw), fw)]
        if kind == "line":
            send(piece, abuf.at[dp, z], a_sem.at[dp, z], dp, line[k] * G + y)
        elif kind == "both":
            send_if(skips(z, line[k]), piece, abuf.at[dp, z], a_sem.at[dp, z], across, line[k] * G + y)
        else:
            send(piece, abuf.at[dp, z], a_sem.at[dp, z], across if kind == "x" else beside, ctx)
    load_w.wait()
    for i in range(2):
        for h in range(heads):
            wloc[i, h] = w_in[:, h, i, :]
        slot, recv = wbuf.at[i, dp, y], w_sem.at[i, dp, y]
        for h in (across, corner):
            send(wloc.at[i, h], slot, recv, h, ctx)
        for h in (dp, beside):
            send(wloc.at[i, h], slot, recv, h, z * G + yo)
        send(wloc.at[i, beside], slot, recv, beside, ctx)
        wbuf[i, dp, y] = wloc[i, dp]
    load_s.wait()
    spbuf[ctx] = jnp.where(
        lax.broadcasted_iota(jnp.int32, spbuf.shape[1:], 0) == 0, span_ref[0], span_ref[1]
    )
    for k in range(Z):
        if k:
            send(spbuf.at[ctx], spbuf.at[ctx], s_sem.at[ctx], dp, line[k] * G + y)
        send(spbuf.at[ctx], spbuf.at[ctx], s_sem.at[ctx], dp, line[k] * G + yo)

    over = z * G + yo
    needed = [None] + [jnp.logical_not(skips(line[k], z)) for k in range(1, Z)]
    ctx_of = [line[k] * G + y for k in range(Z)]

    def relay_w(i):
        for d, far in ((across, 0), (corner, 1)):
            slot, recv = wbuf.at[i, d, y], w_sem.at[i, d, y]
            arrived(slot, recv)
            send(slot, slot, recv, dp, over, name=("w", i, far))

    def relay_z(k):
        slot, recv = abuf.at[dp, line[k]], a_sem.at[dp, line[k]]
        arrived(slot, recv)
        send_if(needed[k], slot, slot, recv, across, ctx, name=("zx", k))
        send(slot, slot, recv, beside, ctx, name=("zc", k))

    def relay_x(k):
        slot, recv = abuf.at[across, line[k]], a_sem.at[across, line[k]]
        arrived(slot, recv)
        send(slot, slot, recv, beside, ctx, name=("xc", k))

    lanes = rsum.shape[2]
    diagonal = lax.broadcasted_iota(jnp.int32, (tokens, lanes), 0) == lax.broadcasted_iota(jnp.int32, (tokens, lanes), 1)

    def project(i, k):
        rows = [abuf[d, line[k]] for d in range(X * C)]
        held = None
        for d in range(X * C):
            part = jnp.dot(rows[d], wbuf[i, d].reshape(fw, hd), preferred_element_type=jnp.float32)
            held = part if held is None else held + part
        return held

    def share(i, k):
        if i == 0:
            for d in (beside, corner):
                arrived(abuf.at[d, line[k]], a_sem.at[d, line[k]])
        if k:
            part = project(i, k)
            if i == 0:
                peak = jnp.maximum(jnp.max(jnp.abs(part), axis=1, keepdims=True), 1e-30)
                part = jnp.round(part * (STEPS / peak)).astype(jnp.int32)
                peaks = jnp.sum(jnp.where(diagonal, peak, 0.0), axis=0, keepdims=True)
                rsum[line[k]] = jnp.broadcast_to(peaks, rsum.shape[1:])
                send(rsum.at[line[k]], rgot.at[z], r_sem.at[z], dp, line[k] * G + y)
            psum[i][line[k]] = part.astype(psum[i].dtype)
            send(psum[i].at[line[k]], got[i].at[z], p_sem.at[i, z], dp, line[k] * G + y)

    def columns(i):
        arrived(wbuf.at[i, beside, y], w_sem.at[i, beside, y])
        for d in (dp, beside, across, corner):
            arrived(wbuf.at[i, d, yo], w_sem.at[i, d, yo])

    relays = {"z": relay_z, "x": relay_x, "w": relay_w}
    for at_z, steps in enumerate(ORDERS):
        @pl.when(z == at_z)
        def _(steps=steps):
            for kind, k in steps:
                relays[kind](k)

    columns(0)
    for k in KEYS:
        share(0, k)
    columns(1)
    for k in VALUES:
        share(1, k)
    copy_a.wait()
    share(0, 0)
    totals = [project(0, 0), project(1, 0)]

    for k in range(Z):
        if k:
            arrived(spbuf.at[line[k] * G + y], s_sem.at[line[k] * G + y])
        arrived(spbuf.at[line[k] * G + yo], s_sem.at[line[k] * G + yo])
    count = Z * G * tokens
    lane = lax.broadcasted_iota(jnp.int32, (1, count), 1)
    key_pos = jnp.zeros((1, count), jnp.int32)
    lanes = spbuf.shape[2]
    for j in range(Z * G):
        for i in range(2):
            base = j * tokens + i * half
            row = spbuf[j, i:i + 1, :]
            row = jnp.concatenate([row] * (count // lanes), axis=1)
            key_pos = jnp.where((lane >= base) & (lane < base + half), row * half + (lane - base), key_pos)
    at = lax.broadcasted_iota(jnp.int32, (tokens, 1), 0)
    own_pos = jnp.where(at < half, span_ref[0] * half + at, span_ref[1] * half + (at - half))
    bias[...] = jnp.where(key_pos <= own_pos, 0.0, -1e30)

    def straight(source, target):
        return (lax.div(2 * source, Z) == lax.div(2 * target, Z)) | ((target == 0) & (c == 0))

    for i in range(2):
        for k in range(1, Z):
            zs = line[k]
            arrived(got[i].at[zs], p_sem.at[i, zs])
            part = got[i][zs].astype(jnp.float32)
            if i == 0:
                arrived(rgot.at[zs], r_sem.at[zs])
                part *= jnp.sum(jnp.where(diagonal, rgot[zs, 0:1, :], 0.0), axis=1, keepdims=True) * (1.0 / STEPS)
            totals[i] += part
        outs[i][ctx] = totals[i].astype(outs[i].dtype)
        mine, recv = outs[i].at[ctx], g_sem.at[i, ctx]
        for kind, k in GATHER:
            if kind == "line":
                send(mine, mine, recv, dp, line[k] * G + y)
            elif k:
                send_if(straight(z, line[k]), mine, mine, recv, dp, line[k] * G + yo)
            else:
                send(mine, mine, recv, dp, z * G + yo)

    def relay(i):
        for k in range(1, Z):
            src = line[k] * G + y
            slot, recv = outs[i].at[src], g_sem.at[i, src]
            arrived(slot, recv)
            send_if(jnp.logical_not(straight(line[k], z)), slot, slot, recv, dp, z * G + yo)

    def gathered(i):
        for k in range(Z):
            src = line[k] * G + yo
            arrived(outs[i].at[src], g_sem.at[i, src])

    load_q.wait()
    relay(0)
    relay(1)
    gathered(0)
    keys = outs[0][...].reshape(count, hd)
    weights, norms = [], []
    for g in range(q_ref.shape[1]):
        query = q_ref[:, g, :]
        score = lax.dot_general(query, keys, (((1,), (1,)), ((), ())), preferred_element_type=jnp.float32)
        score = score * scale + bias[...]
        weight = jnp.exp(score - jnp.max(score, axis=1, keepdims=True))
        norms.append(jnp.sum(weight, axis=1, keepdims=True))
        weights.append(weight.astype(jnp.bfloat16))
    gathered(1)
    values = outs[1][...].reshape(count, hd)
    for g in range(q_ref.shape[1]):
        mixed = jnp.dot(weights[g], values, preferred_element_type=jnp.float32)
        o_ref[:, g * hd:(g + 1) * hd] = (mixed / norms[g]).astype(o_ref.dtype)

    models = (a_ref.at[:, pl.ds(0, fw)], abuf.at[0, 0], wbuf.at[0, 0, 0], psum_k.at[0], psum_v.at[0],
              rsum.at[0], spbuf.at[0])
    models = {(tuple(m.shape), jnp.dtype(m.dtype)): m for m in models}
    for n, want, kind in sent.values():
        wait = remote(models[kind], models[kind], send_sem.at[n], send_sem.at[n], dp, ctx).wait_send
        if want is None:
            wait()
        else:
            pl.when(want)(wait)


def plan(mesh, tokens, shard_rows, heads, head_dim):
    dp, ctx = mesh.shape["dp"], mesh.shape["ctx"]
    if heads != dp or tokens % 16 or tokens > 128 or shard_rows % 16 or head_dim % 128 or (ctx * tokens) % 128:
        return None
    if dp != 4 or ctx != 8 or (2 * shard_rows) % 128:
        return None
    return dp // 2, 2, ctx // 2, 2


def fused(factors, activations, queries, w_kv, span_of):
    X, C, Z, G = factors
    tokens = activations.shape[0]
    shard_rows, heads, _, hd = w_kv.shape
    fw, ctx, dp = G * shard_rows, Z * G, X * C
    group = queries.shape[1]
    dma = pltpu.SemaphoreType.DMA
    bf16, f32 = jnp.bfloat16, jnp.float32
    block = (tokens, hd)
    hbm = pl.BlockSpec(memory_space=pl.ANY)
    sends = 20 * Z + 40
    return pl.pallas_call(
        functools.partial(fused_kernel, X, C, Z, G, 1.0 / math.sqrt(hd)),
        out_shape=pltpu.VMEM((tokens, group * hd), bf16),
        in_specs=[hbm, hbm, hbm, hbm],
        scratch_shapes=[
            pltpu.VMEM(queries.shape, bf16),
            pltpu.VMEM(w_kv.shape, bf16),
            pltpu.VMEM((2, heads, shard_rows, hd), bf16),
            pltpu.VMEM((dp, Z, tokens, fw), bf16),
            pltpu.VMEM((2, dp, G, shard_rows, hd), bf16),
            pltpu.VMEM((Z, *block), jnp.int16),
            pltpu.VMEM((Z, *block), VALUE_PART),
            pltpu.VMEM((Z, *block), jnp.int16),
            pltpu.VMEM((Z, *block), VALUE_PART),
            pltpu.VMEM((Z, 8, 128), f32),
            pltpu.VMEM((Z, 8, 128), f32),
            pltpu.VMEM((ctx, *block), bf16),
            pltpu.VMEM((ctx, *block), bf16),
            pltpu.VMEM((ctx, 8, 128), jnp.int32),
            pltpu.VMEM((tokens, ctx * tokens), f32),
            dma((sends,)), dma((dp, Z)), dma((2, dp, G)), dma((2, Z)), dma((Z,)), dma((2, ctx)), dma((ctx,)), dma((5,)),
            pltpu.SMEM(span_of.shape, jnp.int32),
            pltpu.VMEM(activations.shape, bf16),
        ],
        compiler_params=pltpu.CompilerParams(collective_id=0, has_side_effects=True),
        name="fused",
    )(
        activations,
        queries,
        w_kv,
        span_of,
    )


def attend(carry, keys, values, key_pos, query, query_pos, scale):
    top, total, accum = carry
    score = jnp.einsum("tgd,nd->tgn", query, keys, preferred_element_type=jnp.float32) * scale
    visible = (key_pos[None, :] <= query_pos[:, None])[:, None, :]
    new_top = jnp.maximum(top, jnp.max(jnp.where(visible, score, -1e30), axis=2))
    weight = jnp.where(visible, jnp.exp(score - new_top[..., None]), 0.0)
    factor = jnp.exp(top - new_top)
    total = total * factor + jnp.sum(weight, axis=2)
    accum = accum * factor[..., None] + jnp.einsum(
        "tgn,nd->tgd", weight.astype(jnp.bfloat16), values, preferred_element_type=jnp.float32
    )
    return (new_top, total, accum)


def body(activations, queries, w_kv, span_of, mesh=None):
    factors = plan(mesh, activations.shape[0], w_kv.shape[0], w_kv.shape[1], queries.shape[2])
    if factors is not None:
        return fused(factors, activations, queries, w_kv, span_of)
    tokens = activations.shape[0]
    head_dim = queries.shape[2]
    half = tokens // 2
    scale = 1.0 / math.sqrt(head_dim)
    whole = lax.all_gather(activations, "dp", axis=1, tiled=True)
    shard_rows = w_kv.shape[0]
    mine = lax.all_to_all(w_kv, "dp", split_axis=1, concat_axis=0, tiled=True)
    ordered = whole.reshape(tokens, lax.axis_size("dp"), lax.axis_size("ctx"), shard_rows)
    ordered = jnp.transpose(ordered, (0, 2, 1, 3)).reshape(tokens, -1)
    piece = lax.all_gather(mine, "ctx", axis=0, tiled=True)
    count = piece.shape[0]
    projected = jnp.dot(ordered, piece.reshape(count, -1), preferred_element_type=jnp.float32)
    key_value = projected.astype(jnp.bfloat16).reshape(tokens, 2, head_dim)
    all_spans = lax.all_gather(span_of, "ctx", axis=0, tiled=True)
    offsets = jnp.arange(tokens, dtype=jnp.int32)
    own_pos = jnp.where(offsets < half, span_of[0], span_of[1]) * half + offsets % half

    def update(state, part, part_pos):
        return attend(state, part[:, 0], part[:, 1], part_pos, queries, own_pos, scale)

    group = queries.shape[1]
    start_state = (
        jnp.full((tokens, group), -1e30, jnp.float32),
        jnp.zeros((tokens, group), jnp.float32),
        jnp.zeros((tokens, group, head_dim), jnp.float32),
    )
    state = start_state
    piece = lax.all_gather(key_value, "ctx", axis=0, tiled=True)
    count = piece.shape[0]
    index = jnp.arange(count, dtype=jnp.int32)
    key_pos = jnp.take(all_spans, index // half) * half + index % half
    block = 1024 if count % 1024 == 0 else count

    def step(held, item):
        return (update(held, item[0], item[1]), None)

    blocks = (
        piece.reshape(count // block, block, 2, head_dim),
        key_pos.reshape(count // block, block),
    )
    state, _ = lax.scan(step, state, blocks)
    top, total, accum = state
    return (accum / total[..., None]).astype(jnp.bfloat16).reshape(tokens, group * head_dim)


def solution(mesh):
    return jax.shard_map(
        functools.partial(body, mesh=mesh),
        mesh=mesh,
        in_specs=(
            P("ctx", "dp"),
            P("ctx", "dp", None),
            P(("dp", "ctx"), None, None, None),
            P("ctx"),
        ),
        out_specs=P("ctx", "dp"),
        check_vma=False,
    )
```

```python
import functools
import math

import jax
import jax.numpy as jnp
from jax import lax
from jax.experimental import pallas as pl
from jax.experimental.pallas import tpu as pltpu
from jax.sharding import PartitionSpec as P

MESH = pl.DeviceIdType.MESH
VALUE_PART = jnp.bfloat16
STEPS = 32767.0
ORDERS = ((('z', 1), ('x', 1), ('x', 0), ('z', 2), ('w', 0), ('z', 3), ('w', 1), ('x', 3), ('x', 2)), (('z', 1), ('x', 0), ('w', 0), ('z', 3), ('z', 2), ('x', 1), ('w', 1), ('x', 2), ('x', 3)), (('z', 2), ('z', 1), ('x', 0), ('w', 0), ('z', 3), ('x', 1), ('w', 1), ('x', 2), ('x', 3)), (('z', 1), ('x', 0), ('z', 2), ('w', 0), ('z', 3), ('x', 1), ('w', 1), ('x', 2), ('x', 3)))
FIRST = (('line', 1), ('line', 2), ('line', 3), ('both', 1), ('both', 2), ('core', 0), ('both', 3), ('x', 0))
GATHER = (('line', 3), ('over', 3), ('over', 2), ('line', 2), ('line', 1), ('over', 0), ('over', 1))
KEYS = (1, 2, 3)
VALUES = (1, 2, 3)


def remote(src, dst, send, recv, dp, ctx):
    return pltpu.make_async_remote_copy(
        src_ref=src,
        dst_ref=dst,
        send_sem=send,
        recv_sem=recv,
        device_id={"dp": dp, "ctx": ctx},
        device_id_type=MESH,
    )


def fused_kernel(
    X, C, Z, G, scale,
    a_hbm, q_in, w_hbm, span_in, o_ref,
    q_ref, w_in, wloc, abuf, wbuf, psum_k, psum_v, got_k, got_v, rsum, rgot, kbuf, vbuf, spbuf, bias,
    send_sem, a_sem, w_sem, p_sem, r_sem, g_sem, s_sem, own_sem, span_ref, a_ref,
):
    dp, ctx = lax.axis_index("dp"), lax.axis_index("ctx")
    x, c = lax.div(dp, C), lax.rem(dp, C)
    z, y = lax.div(ctx, G), lax.rem(ctx, G)
    tokens = a_ref.shape[0]
    half = tokens // 2
    fw, hd = abuf.shape[3], kbuf.shape[2]
    heads = w_in.shape[1]
    psum, got, outs = (psum_k, psum_v), (got_k, got_v), (kbuf, vbuf)
    xo, co, yo = X - 1 - x, C - 1 - c, G - 1 - y
    across, beside, corner = xo * C + c, x * C + co, xo * C + co

    way = 1 - 2 * lax.div(2 * z, Z)
    edge = (z == 0) | (z == Z - 1)
    line = [z, z + way, jnp.where(edge, z + 2 * way, z - way), jnp.where(edge, z + 3 * way, z + 2 * way)]

    def arrived(slot, recv):
        remote(slot, slot, recv, recv, dp, ctx).wait_recv()

    sent = {}

    def send(src, dst, recv, to_dp, to_ctx, want=None, name=None):
        key = len(sent) if name is None else name
        n = sent.setdefault(key, (len(sent), want, (tuple(src.shape), jnp.dtype(src.dtype))))[0]
        copy = remote(src, dst, send_sem.at[n], recv, to_dp, to_ctx)
        if want is None:
            copy.start()
        else:
            pl.when(want)(copy.start)

    def send_if(want, *args, **kwargs):
        send(*args, want=want, **kwargs)

    peers = [(dp, line[k] * G + y) for k in range(1, Z)]
    peers += [(dp, line[k] * G + yo) for k in range(Z)]
    peers += [(beside, z * G + yo), (across, ctx), (beside, ctx), (corner, ctx)]
    peers += [(across, line[k] * G + y) for k in range(1, Z)]

    def skips(source, target):
        return (jnp.abs(source - target) == Z - 1) | ((jnp.abs(source - target) == 1) & (source + target != Z - 1))

    load_w = pltpu.make_async_copy(w_hbm, w_in, own_sem.at[2])
    load_q = pltpu.make_async_copy(q_in, q_ref, own_sem.at[3])
    load_a = pltpu.make_async_copy(a_hbm, a_ref, own_sem.at[4])
    barrier = pltpu.get_barrier_semaphore()
    for pd, pc in peers:
        pl.semaphore_signal(barrier, inc=1, device_id={"dp": pd, "ctx": pc}, device_id_type=MESH)
    load_s = pltpu.make_async_copy(span_in, span_ref, own_sem.at[1])
    load_a.start()
    load_w.start()
    load_s.start()
    own_a = a_ref.at[:, pl.ds(pl.multiple_of(z * fw, fw), fw)]
    copy_a = pltpu.make_async_copy(own_a, abuf.at[dp, z], own_sem.at[0])
    load_q.start()
    pl.semaphore_wait(barrier, len(peers))
    load_a.wait()
    copy_a.start()

    for kind, k in FIRST:
        piece = a_ref.at[:, pl.ds(pl.multiple_of(line[k] * fw, fw), fw)]
        if kind == "line":
            send(piece, abuf.at[dp, z], a_sem.at[dp, z], dp, line[k] * G + y)
        elif kind == "both":
            send_if(skips(z, line[k]), piece, abuf.at[dp, z], a_sem.at[dp, z], across, line[k] * G + y)
        else:
            send(piece, abuf.at[dp, z], a_sem.at[dp, z], across if kind == "x" else beside, ctx)
    load_w.wait()
    for i in range(2):
        for h in range(heads):
            wloc[i, h] = w_in[:, h, i, :]
        slot, recv = wbuf.at[i, dp, y], w_sem.at[i, dp, y]
        for h in (across, corner):
            send(wloc.at[i, h], slot, recv, h, ctx)
        for h in (dp, beside):
            send(wloc.at[i, h], slot, recv, h, z * G + yo)
        send(wloc.at[i, beside], slot, recv, beside, ctx)
        wbuf[i, dp, y] = wloc[i, dp]
    load_s.wait()
    spbuf[ctx] = jnp.where(
        lax.broadcasted_iota(jnp.int32, spbuf.shape[1:], 0) == 0, span_ref[0], span_ref[1]
    )
    for k in range(Z):
        if k:
            send(spbuf.at[ctx], spbuf.at[ctx], s_sem.at[ctx], dp, line[k] * G + y)
        send(spbuf.at[ctx], spbuf.at[ctx], s_sem.at[ctx], dp, line[k] * G + yo)

    over = z * G + yo
    needed = [None] + [jnp.logical_not(skips(line[k], z)) for k in range(1, Z)]
    ctx_of = [line[k] * G + y for k in range(Z)]

    def relay_w(i):
        for d, far in ((across, 0), (corner, 1)):
            slot, recv = wbuf.at[i, d, y], w_sem.at[i, d, y]
            arrived(slot, recv)
            send(slot, slot, recv, dp, over, name=("w", i, far))

    def relay_z(k):
        slot, recv = abuf.at[dp, line[k]], a_sem.at[dp, line[k]]
        arrived(slot, recv)
        send_if(needed[k], slot, slot, recv, across, ctx, name=("zx", k))
        send(slot, slot, recv, beside, ctx, name=("zc", k))

    def relay_x(k):
        slot, recv = abuf.at[across, line[k]], a_sem.at[across, line[k]]
        arrived(slot, recv)
        send(slot, slot, recv, beside, ctx, name=("xc", k))

    lanes = rsum.shape[2]
    diagonal = lax.broadcasted_iota(jnp.int32, (tokens, lanes), 0) == lax.broadcasted_iota(jnp.int32, (tokens, lanes), 1)

    def project(i, k):
        rows = [abuf[d, line[k]] for d in range(X * C)]
        held = None
        for d in range(X * C):
            part = jnp.dot(rows[d], wbuf[i, d].reshape(fw, hd), preferred_element_type=jnp.float32)
            held = part if held is None else held + part
        return held

    def share(i, k):
        if i == 0:
            for d in (beside, corner):
                arrived(abuf.at[d, line[k]], a_sem.at[d, line[k]])
        if k:
            part = project(i, k)
            if i == 0:
                peak = jnp.maximum(jnp.max(jnp.abs(part), axis=1, keepdims=True), 1e-30)
                part = jnp.round(part * (STEPS / peak)).astype(jnp.int32)
                peaks = jnp.sum(jnp.where(diagonal, peak, 0.0), axis=0, keepdims=True)
                rsum[line[k]] = jnp.broadcast_to(peaks, rsum.shape[1:])
                send(rsum.at[line[k]], rgot.at[z], r_sem.at[z], dp, line[k] * G + y)
            psum[i][line[k]] = part.astype(psum[i].dtype)
            send(psum[i].at[line[k]], got[i].at[z], p_sem.at[i, z], dp, line[k] * G + y)

    def columns(i):
        arrived(wbuf.at[i, beside, y], w_sem.at[i, beside, y])
        for d in (dp, beside, across, corner):
            arrived(wbuf.at[i, d, yo], w_sem.at[i, d, yo])

    relays = {"z": relay_z, "x": relay_x, "w": relay_w}
    for at_z, steps in enumerate(ORDERS):
        @pl.when(z == at_z)
        def _(steps=steps):
            for kind, k in steps:
                relays[kind](k)

    columns(0)
    for k in KEYS:
        share(0, k)
    columns(1)
    for k in VALUES:
        share(1, k)
    copy_a.wait()
    share(0, 0)
    totals = [project(0, 0), project(1, 0)]

    for k in range(Z):
        if k:
            arrived(spbuf.at[line[k] * G + y], s_sem.at[line[k] * G + y])
        arrived(spbuf.at[line[k] * G + yo], s_sem.at[line[k] * G + yo])
    count = Z * G * tokens
    lane = lax.broadcasted_iota(jnp.int32, (1, count), 1)
    key_pos = jnp.zeros((1, count), jnp.int32)
    lanes = spbuf.shape[2]
    for j in range(Z * G):
        for i in range(2):
            base = j * tokens + i * half
            row = spbuf[j, i:i + 1, :]
            row = jnp.concatenate([row] * (count // lanes), axis=1)
            key_pos = jnp.where((lane >= base) & (lane < base + half), row * half + (lane - base), key_pos)
    at = lax.broadcasted_iota(jnp.int32, (tokens, 1), 0)
    own_pos = jnp.where(at < half, span_ref[0] * half + at, span_ref[1] * half + (at - half))
    bias[...] = jnp.where(key_pos <= own_pos, 0.0, -1e30)

    def straight(source, target):
        return (c == 0) & (((source == 0) & (target == 1)) | (target == 0))

    for i in range(2):
        for k in range(1, Z):
            zs = line[k]
            arrived(got[i].at[zs], p_sem.at[i, zs])
            part = got[i][zs].astype(jnp.float32)
            if i == 0:
                arrived(rgot.at[zs], r_sem.at[zs])
                part *= jnp.sum(jnp.where(diagonal, rgot[zs, 0:1, :], 0.0), axis=1, keepdims=True) * (1.0 / STEPS)
            totals[i] += part
        outs[i][ctx] = totals[i].astype(outs[i].dtype)
        mine, recv = outs[i].at[ctx], g_sem.at[i, ctx]
        for kind, k in GATHER:
            if kind == "line":
                send(mine, mine, recv, dp, line[k] * G + y)
            elif k:
                send_if(straight(z, line[k]), mine, mine, recv, dp, line[k] * G + yo)
            else:
                send(mine, mine, recv, dp, z * G + yo)

    def relay(i):
        for k in range(1, Z):
            src = line[k] * G + y
            slot, recv = outs[i].at[src], g_sem.at[i, src]
            arrived(slot, recv)
            send_if(jnp.logical_not(straight(line[k], z)), slot, slot, recv, dp, z * G + yo)

    def gathered(i):
        for k in range(Z):
            src = line[k] * G + yo
            arrived(outs[i].at[src], g_sem.at[i, src])

    load_q.wait()
    relay(0)
    relay(1)
    gathered(0)
    keys = outs[0][...].reshape(count, hd)
    weights, norms = [], []
    for g in range(q_ref.shape[1]):
        query = q_ref[:, g, :]
        score = lax.dot_general(query, keys, (((1,), (1,)), ((), ())), preferred_element_type=jnp.float32)
        score = score * scale + bias[...]
        weight = jnp.exp(score - jnp.max(score, axis=1, keepdims=True))
        norms.append(1.0 / jnp.sum(weight, axis=1, keepdims=True))
        weights.append(weight.astype(jnp.bfloat16))
    gathered(1)
    values = outs[1][...].reshape(count, hd)
    for g in range(q_ref.shape[1]):
        mixed = jnp.dot(weights[g], values, preferred_element_type=jnp.float32)
        o_ref[:, g * hd:(g + 1) * hd] = (mixed * norms[g]).astype(o_ref.dtype)

    models = (a_ref.at[:, pl.ds(0, fw)], abuf.at[0, 0], wbuf.at[0, 0, 0], psum_k.at[0], psum_v.at[0],
              rsum.at[0], spbuf.at[0])
    models = {(tuple(m.shape), jnp.dtype(m.dtype)): m for m in models}
    for n, want, kind in sent.values():
        wait = remote(models[kind], models[kind], send_sem.at[n], send_sem.at[n], dp, ctx).wait_send
        if want is None:
            wait()
        else:
            pl.when(want)(wait)


def plan(mesh, tokens, shard_rows, heads, head_dim):
    dp, ctx = mesh.shape["dp"], mesh.shape["ctx"]
    if heads != dp or tokens % 16 or tokens > 128 or shard_rows % 16 or head_dim % 128 or (ctx * tokens) % 128:
        return None
    if dp != 4 or ctx != 8 or (2 * shard_rows) % 128:
        return None
    return dp // 2, 2, ctx // 2, 2


def fused(factors, activations, queries, w_kv, span_of):
    X, C, Z, G = factors
    tokens = activations.shape[0]
    shard_rows, heads, _, hd = w_kv.shape
    fw, ctx, dp = G * shard_rows, Z * G, X * C
    group = queries.shape[1]
    dma = pltpu.SemaphoreType.DMA
    bf16, f32 = jnp.bfloat16, jnp.float32
    block = (tokens, hd)
    hbm = pl.BlockSpec(memory_space=pl.ANY)
    sends = 20 * Z + 40
    return pl.pallas_call(
        functools.partial(fused_kernel, X, C, Z, G, 1.0 / math.sqrt(hd)),
        out_shape=pltpu.VMEM((tokens, group * hd), bf16),
        in_specs=[hbm, hbm, hbm, hbm],
        scratch_shapes=[
            pltpu.VMEM(queries.shape, bf16),
            pltpu.VMEM(w_kv.shape, bf16),
            pltpu.VMEM((2, heads, shard_rows, hd), bf16),
            pltpu.VMEM((dp, Z, tokens, fw), bf16),
            pltpu.VMEM((2, dp, G, shard_rows, hd), bf16),
            pltpu.VMEM((Z, *block), jnp.int16),
            pltpu.VMEM((Z, *block), VALUE_PART),
            pltpu.VMEM((Z, *block), jnp.int16),
            pltpu.VMEM((Z, *block), VALUE_PART),
            pltpu.VMEM((Z, 8, 128), f32),
            pltpu.VMEM((Z, 8, 128), f32),
            pltpu.VMEM((ctx, *block), bf16),
            pltpu.VMEM((ctx, *block), bf16),
            pltpu.VMEM((ctx, 8, 128), jnp.int32),
            pltpu.VMEM((tokens, ctx * tokens), f32),
            dma((sends,)), dma((dp, Z)), dma((2, dp, G)), dma((2, Z)), dma((Z,)), dma((2, ctx)), dma((ctx,)), dma((5,)),
            pltpu.SMEM(span_of.shape, jnp.int32),
            pltpu.VMEM(activations.shape, bf16),
        ],
        compiler_params=pltpu.CompilerParams(collective_id=0, has_side_effects=True),
        name="fused",
    )(
        activations,
        queries,
        w_kv,
        span_of,
    )


def attend(carry, keys, values, key_pos, query, query_pos, scale):
    top, total, accum = carry
    score = jnp.einsum("tgd,nd->tgn", query, keys, preferred_element_type=jnp.float32) * scale
    visible = (key_pos[None, :] <= query_pos[:, None])[:, None, :]
    new_top = jnp.maximum(top, jnp.max(jnp.where(visible, score, -1e30), axis=2))
    weight = jnp.where(visible, jnp.exp(score - new_top[..., None]), 0.0)
    factor = jnp.exp(top - new_top)
    total = total * factor + jnp.sum(weight, axis=2)
    accum = accum * factor[..., None] + jnp.einsum(
        "tgn,nd->tgd", weight.astype(jnp.bfloat16), values, preferred_element_type=jnp.float32
    )
    return (new_top, total, accum)


def body(activations, queries, w_kv, span_of, mesh=None):
    factors = plan(mesh, activations.shape[0], w_kv.shape[0], w_kv.shape[1], queries.shape[2])
    if factors is not None:
        return fused(factors, activations, queries, w_kv, span_of)
    tokens = activations.shape[0]
    head_dim = queries.shape[2]
    half = tokens // 2
    scale = 1.0 / math.sqrt(head_dim)
    whole = lax.all_gather(activations, "dp", axis=1, tiled=True)
    shard_rows = w_kv.shape[0]
    mine = lax.all_to_all(w_kv, "dp", split_axis=1, concat_axis=0, tiled=True)
    ordered = whole.reshape(tokens, lax.axis_size("dp"), lax.axis_size("ctx"), shard_rows)
    ordered = jnp.transpose(ordered, (0, 2, 1, 3)).reshape(tokens, -1)
    piece = lax.all_gather(mine, "ctx", axis=0, tiled=True)
    count = piece.shape[0]
    projected = jnp.dot(ordered, piece.reshape(count, -1), preferred_element_type=jnp.float32)
    key_value = projected.astype(jnp.bfloat16).reshape(tokens, 2, head_dim)
    all_spans = lax.all_gather(span_of, "ctx", axis=0, tiled=True)
    offsets = jnp.arange(tokens, dtype=jnp.int32)
    own_pos = jnp.where(offsets < half, span_of[0], span_of[1]) * half + offsets % half

    def update(state, part, part_pos):
        return attend(state, part[:, 0], part[:, 1], part_pos, queries, own_pos, scale)

    group = queries.shape[1]
    start_state = (
        jnp.full((tokens, group), -1e30, jnp.float32),
        jnp.zeros((tokens, group), jnp.float32),
        jnp.zeros((tokens, group, head_dim), jnp.float32),
    )
    state = start_state
    piece = lax.all_gather(key_value, "ctx", axis=0, tiled=True)
    count = piece.shape[0]
    index = jnp.arange(count, dtype=jnp.int32)
    key_pos = jnp.take(all_spans, index // half) * half + index % half
    block = 1024 if count % 1024 == 0 else count

    def step(held, item):
        return (update(held, item[0], item[1]), None)

    blocks = (
        piece.reshape(count // block, block, 2, head_dim),
        key_pos.reshape(count // block, block),
    )
    state, _ = lax.scan(step, state, blocks)
    top, total, accum = state
    return (accum / total[..., None]).astype(jnp.bfloat16).reshape(tokens, group * head_dim)


def solution(mesh):
    return jax.shard_map(
        functools.partial(body, mesh=mesh),
        mesh=mesh,
        in_specs=(
            P("ctx", "dp"),
            P("ctx", "dp", None),
            P(("dp", "ctx"), None, None, None),
            P("ctx"),
        ),
        out_specs=P("ctx", "dp"),
        check_vma=False,
    )
```

```python
import functools
import math

import jax
import jax.numpy as jnp
from jax import lax
from jax.experimental import pallas as pl
from jax.experimental.pallas import tpu as pltpu
from jax.sharding import PartitionSpec as P

MESH = pl.DeviceIdType.MESH
VALUE_PART = jnp.bfloat16
STEPS = 32767.0
ORDERS = ((('z', 1), ('x', 1), ('x', 0), ('z', 2), ('w', 0), ('z', 3), ('w', 1), ('x', 3), ('x', 2)), (('z', 1), ('x', 0), ('w', 0), ('z', 3), ('z', 2), ('x', 1), ('w', 1), ('x', 2), ('x', 3)), (('z', 2), ('z', 1), ('x', 0), ('w', 0), ('z', 3), ('x', 1), ('w', 1), ('x', 2), ('x', 3)), (('z', 1), ('x', 0), ('z', 2), ('w', 0), ('z', 3), ('x', 1), ('w', 1), ('x', 2), ('x', 3)))
FIRST = (('line', 1), ('line', 2), ('line', 3), ('both', 1), ('both', 2), ('core', 0), ('both', 3), ('x', 0))
GATHER = (('line', 3), ('over', 3), ('over', 2), ('line', 2), ('line', 1), ('over', 0), ('over', 1))
KEYS = (1, 2, 3)
VALUES = (1, 2, 3)


def remote(src, dst, send, recv, dp, ctx):
    return pltpu.make_async_remote_copy(
        src_ref=src,
        dst_ref=dst,
        send_sem=send,
        recv_sem=recv,
        device_id={"dp": dp, "ctx": ctx},
        device_id_type=MESH,
    )


def fused_kernel(
    X, C, Z, G, scale,
    a_hbm, q_in, w_hbm, span_in, o_ref,
    q_ref, w_in, wloc, abuf, wbuf, psum_k, psum_v, got_k, got_v, rsum, rgot, kbuf, vbuf, spbuf, bias,
    send_sem, a_sem, w_sem, p_sem, r_sem, g_sem, s_sem, own_sem, span_ref, a_ref,
):
    dp, ctx = lax.axis_index("dp"), lax.axis_index("ctx")
    x, c = lax.div(dp, C), lax.rem(dp, C)
    z, y = lax.div(ctx, G), lax.rem(ctx, G)
    tokens = a_ref.shape[0]
    half = tokens // 2
    fw, hd = abuf.shape[3], kbuf.shape[2]
    heads = w_in.shape[1]
    psum, got, outs = (psum_k, psum_v), (got_k, got_v), (kbuf, vbuf)
    xo, co, yo = X - 1 - x, C - 1 - c, G - 1 - y
    across, beside, corner = xo * C + c, x * C + co, xo * C + co

    way = 1 - 2 * lax.div(2 * z, Z)
    edge = (z == 0) | (z == Z - 1)
    line = [z, z + way, jnp.where(edge, z + 2 * way, z - way), jnp.where(edge, z + 3 * way, z + 2 * way)]

    def arrived(slot, recv):
        remote(slot, slot, recv, recv, dp, ctx).wait_recv()

    sent = {}

    def send(src, dst, recv, to_dp, to_ctx, want=None, name=None):
        key = len(sent) if name is None else name
        n = sent.setdefault(key, (len(sent), want, (tuple(src.shape), jnp.dtype(src.dtype))))[0]
        copy = remote(src, dst, send_sem.at[n], recv, to_dp, to_ctx)
        if want is None:
            copy.start()
        else:
            pl.when(want)(copy.start)

    def send_if(want, *args, **kwargs):
        send(*args, want=want, **kwargs)

    peers = [(dp, line[k] * G + y) for k in range(1, Z)]
    peers += [(dp, line[k] * G + yo) for k in range(Z)]
    peers += [(beside, z * G + yo), (across, ctx), (beside, ctx), (corner, ctx)]
    peers += [(across, line[k] * G + y) for k in range(1, Z)]

    def skips(source, target):
        return (jnp.abs(source - target) == Z - 1) | ((jnp.abs(source - target) == 1) & (source + target != Z - 1))

    load_w = pltpu.make_async_copy(w_hbm, w_in, own_sem.at[2])
    load_q = pltpu.make_async_copy(q_in, q_ref, own_sem.at[3])
    load_a = pltpu.make_async_copy(a_hbm, a_ref, own_sem.at[4])
    barrier = pltpu.get_barrier_semaphore()
    for pd, pc in peers:
        pl.semaphore_signal(barrier, inc=1, device_id={"dp": pd, "ctx": pc}, device_id_type=MESH)
    load_s = pltpu.make_async_copy(span_in, span_ref, own_sem.at[1])
    load_a.start()
    load_w.start()
    load_s.start()
    own_a = a_ref.at[:, pl.ds(pl.multiple_of(z * fw, fw), fw)]
    copy_a = pltpu.make_async_copy(own_a, abuf.at[dp, z], own_sem.at[0])
    load_q.start()
    pl.semaphore_wait(barrier, len(peers))
    load_a.wait()
    copy_a.start()

    for kind, k in FIRST:
        piece = a_ref.at[:, pl.ds(pl.multiple_of(line[k] * fw, fw), fw)]
        if kind == "line":
            send(piece, abuf.at[dp, z], a_sem.at[dp, z], dp, line[k] * G + y)
        elif kind == "both":
            send_if(skips(z, line[k]), piece, abuf.at[dp, z], a_sem.at[dp, z], across, line[k] * G + y)
        else:
            send(piece, abuf.at[dp, z], a_sem.at[dp, z], across if kind == "x" else beside, ctx)
    load_w.wait()
    for i in range(2):
        for h in range(heads):
            wloc[i, h] = w_in[:, h, i, :]
        slot, recv = wbuf.at[i, dp, y], w_sem.at[i, dp, y]
        for h in (across, corner):
            send(wloc.at[i, h], slot, recv, h, ctx)
        for h in (dp, beside):
            send(wloc.at[i, h], slot, recv, h, z * G + yo)
        send(wloc.at[i, beside], slot, recv, beside, ctx)
        wbuf[i, dp, y] = wloc[i, dp]
    load_s.wait()
    spbuf[ctx] = jnp.where(
        lax.broadcasted_iota(jnp.int32, spbuf.shape[1:], 0) == 0, span_ref[0], span_ref[1]
    )
    for k in range(Z):
        if k:
            send(spbuf.at[ctx], spbuf.at[ctx], s_sem.at[ctx], dp, line[k] * G + y)
        send(spbuf.at[ctx], spbuf.at[ctx], s_sem.at[ctx], dp, line[k] * G + yo)

    over = z * G + yo
    needed = [None] + [jnp.logical_not(skips(line[k], z)) for k in range(1, Z)]
    ctx_of = [line[k] * G + y for k in range(Z)]

    def relay_w(i):
        for d, far in ((across, 0), (corner, 1)):
            slot, recv = wbuf.at[i, d, y], w_sem.at[i, d, y]
            arrived(slot, recv)
            send(slot, slot, recv, dp, over, name=("w", i, far))

    def relay_z(k):
        slot, recv = abuf.at[dp, line[k]], a_sem.at[dp, line[k]]
        arrived(slot, recv)
        send_if(needed[k], slot, slot, recv, across, ctx, name=("zx", k))
        send(slot, slot, recv, beside, ctx, name=("zc", k))

    def relay_x(k):
        slot, recv = abuf.at[across, line[k]], a_sem.at[across, line[k]]
        arrived(slot, recv)
        send(slot, slot, recv, beside, ctx, name=("xc", k))

    lanes = rsum.shape[2]
    diagonal = lax.broadcasted_iota(jnp.int32, (tokens, lanes), 0) == lax.broadcasted_iota(jnp.int32, (tokens, lanes), 1)

    def project(i, k):
        rows = [abuf[d, line[k]] for d in range(X * C)]
        held = None
        for d in range(X * C):
            part = jnp.dot(rows[d], wbuf[i, d].reshape(fw, hd), preferred_element_type=jnp.float32)
            held = part if held is None else held + part
        return held

    def share(i, k):
        if i == 0:
            for d in (beside, corner):
                arrived(abuf.at[d, line[k]], a_sem.at[d, line[k]])
        if k:
            part = project(i, k)
            if i == 0:
                peak = jnp.maximum(jnp.max(jnp.abs(part), axis=1, keepdims=True), 1e-30)
                part = jnp.round(part * (STEPS / peak)).astype(jnp.int32)
                peaks = jnp.sum(jnp.where(diagonal, peak, 0.0), axis=0, keepdims=True)
                rsum[line[k]] = jnp.broadcast_to(peaks, rsum.shape[1:])
                send(rsum.at[line[k]], rgot.at[z], r_sem.at[z], dp, line[k] * G + y)
            psum[i][line[k]] = part.astype(psum[i].dtype)
            send(psum[i].at[line[k]], got[i].at[z], p_sem.at[i, z], dp, line[k] * G + y)

    def columns(i):
        arrived(wbuf.at[i, beside, y], w_sem.at[i, beside, y])
        for d in (dp, beside, across, corner):
            arrived(wbuf.at[i, d, yo], w_sem.at[i, d, yo])

    relays = {"z": relay_z, "x": relay_x, "w": relay_w}
    for at_z, steps in enumerate(ORDERS):
        @pl.when(z == at_z)
        def _(steps=steps):
            for kind, k in steps:
                relays[kind](k)

    columns(0)
    for k in KEYS:
        share(0, k)
    columns(1)
    for k in VALUES:
        share(1, k)
    copy_a.wait()
    share(0, 0)
    totals = [project(0, 0), project(1, 0)]

    for k in range(Z):
        if k:
            arrived(spbuf.at[line[k] * G + y], s_sem.at[line[k] * G + y])
        arrived(spbuf.at[line[k] * G + yo], s_sem.at[line[k] * G + yo])
    count = Z * G * tokens
    lane = lax.broadcasted_iota(jnp.int32, (1, count), 1)
    key_pos = jnp.zeros((1, count), jnp.int32)
    lanes = spbuf.shape[2]
    for j in range(Z * G):
        for i in range(2):
            base = j * tokens + i * half
            row = spbuf[j, i:i + 1, :]
            row = jnp.concatenate([row] * (count // lanes), axis=1)
            key_pos = jnp.where((lane >= base) & (lane < base + half), row * half + (lane - base), key_pos)
    at = lax.broadcasted_iota(jnp.int32, (tokens, 1), 0)
    own_pos = jnp.where(at < half, span_ref[0] * half + at, span_ref[1] * half + (at - half))
    bias[...] = jnp.where(key_pos <= own_pos, 0.0, -1e30)

    def straight(source, target):
        return (c == 0) & (((source == 0) & (target == 1)) | (target == 0))

    for i in range(2):
        for k in range(1, Z):
            zs = line[k]
            arrived(got[i].at[zs], p_sem.at[i, zs])
            part = got[i][zs].astype(jnp.float32)
            if i == 0:
                arrived(rgot.at[zs], r_sem.at[zs])
                part *= jnp.sum(jnp.where(diagonal, rgot[zs, 0:1, :], 0.0), axis=1, keepdims=True) * (1.0 / STEPS)
            totals[i] += part
        outs[i][ctx] = totals[i].astype(outs[i].dtype)
        mine, recv = outs[i].at[ctx], g_sem.at[i, ctx]
        for kind, k in GATHER:
            if kind == "line":
                send(mine, mine, recv, dp, line[k] * G + y)
            elif k:
                send_if(straight(z, line[k]), mine, mine, recv, dp, line[k] * G + yo)
            else:
                send(mine, mine, recv, dp, z * G + yo)

    def relay(i):
        for k in (3, 2, 1):
            src = line[k] * G + y
            slot, recv = outs[i].at[src], g_sem.at[i, src]
            arrived(slot, recv)
            send_if(jnp.logical_not(straight(line[k], z)), slot, slot, recv, dp, z * G + yo)

    def gathered(i):
        for k in range(Z):
            src = line[k] * G + yo
            arrived(outs[i].at[src], g_sem.at[i, src])

    load_q.wait()
    relay(0)
    relay(1)
    gathered(0)
    keys = outs[0][...].reshape(count, hd)
    weights, norms = [], []
    for g in range(q_ref.shape[1]):
        query = q_ref[:, g, :]
        score = lax.dot_general(query, keys, (((1,), (1,)), ((), ())), preferred_element_type=jnp.float32)
        score = score * scale + bias[...]
        weight = jnp.exp(score - jnp.max(score, axis=1, keepdims=True))
        norms.append(1.0 / jnp.sum(weight, axis=1, keepdims=True))
        weights.append(weight.astype(jnp.bfloat16))
    gathered(1)
    values = outs[1][...].reshape(count, hd)
    for g in range(q_ref.shape[1]):
        mixed = jnp.dot(weights[g], values, preferred_element_type=jnp.float32)
        o_ref[:, g * hd:(g + 1) * hd] = (mixed * norms[g]).astype(o_ref.dtype)

    models = (a_ref.at[:, pl.ds(0, fw)], abuf.at[0, 0], wbuf.at[0, 0, 0], psum_k.at[0], psum_v.at[0],
              rsum.at[0], spbuf.at[0])
    models = {(tuple(m.shape), jnp.dtype(m.dtype)): m for m in models}
    for n, want, kind in sent.values():
        wait = remote(models[kind], models[kind], send_sem.at[n], send_sem.at[n], dp, ctx).wait_send
        if want is None:
            wait()
        else:
            pl.when(want)(wait)


def plan(mesh, tokens, shard_rows, heads, head_dim):
    dp, ctx = mesh.shape["dp"], mesh.shape["ctx"]
    if heads != dp or tokens % 16 or tokens > 128 or shard_rows % 16 or head_dim % 128 or (ctx * tokens) % 128:
        return None
    if dp != 4 or ctx != 8 or (2 * shard_rows) % 128:
        return None
    return dp // 2, 2, ctx // 2, 2


def fused(factors, activations, queries, w_kv, span_of):
    X, C, Z, G = factors
    tokens = activations.shape[0]
    shard_rows, heads, _, hd = w_kv.shape
    fw, ctx, dp = G * shard_rows, Z * G, X * C
    group = queries.shape[1]
    dma = pltpu.SemaphoreType.DMA
    bf16, f32 = jnp.bfloat16, jnp.float32
    block = (tokens, hd)
    hbm = pl.BlockSpec(memory_space=pl.ANY)
    sends = 20 * Z + 40
    return pl.pallas_call(
        functools.partial(fused_kernel, X, C, Z, G, 1.0 / math.sqrt(hd)),
        out_shape=pltpu.VMEM((tokens, group * hd), bf16),
        in_specs=[hbm, hbm, hbm, hbm],
        scratch_shapes=[
            pltpu.VMEM(queries.shape, bf16),
            pltpu.VMEM(w_kv.shape, bf16),
            pltpu.VMEM((2, heads, shard_rows, hd), bf16),
            pltpu.VMEM((dp, Z, tokens, fw), bf16),
            pltpu.VMEM((2, dp, G, shard_rows, hd), bf16),
            pltpu.VMEM((Z, *block), jnp.int16),
            pltpu.VMEM((Z, *block), VALUE_PART),
            pltpu.VMEM((Z, *block), jnp.int16),
            pltpu.VMEM((Z, *block), VALUE_PART),
            pltpu.VMEM((Z, 8, 128), f32),
            pltpu.VMEM((Z, 8, 128), f32),
            pltpu.VMEM((ctx, *block), bf16),
            pltpu.VMEM((ctx, *block), bf16),
            pltpu.VMEM((ctx, 8, 128), jnp.int32),
            pltpu.VMEM((tokens, ctx * tokens), f32),
            dma((sends,)), dma((dp, Z)), dma((2, dp, G)), dma((2, Z)), dma((Z,)), dma((2, ctx)), dma((ctx,)), dma((5,)),
            pltpu.SMEM(span_of.shape, jnp.int32),
            pltpu.VMEM(activations.shape, bf16),
        ],
        compiler_params=pltpu.CompilerParams(collective_id=0, has_side_effects=True),
        name="fused",
    )(
        activations,
        queries,
        w_kv,
        span_of,
    )


def attend(carry, keys, values, key_pos, query, query_pos, scale):
    top, total, accum = carry
    score = jnp.einsum("tgd,nd->tgn", query, keys, preferred_element_type=jnp.float32) * scale
    visible = (key_pos[None, :] <= query_pos[:, None])[:, None, :]
    new_top = jnp.maximum(top, jnp.max(jnp.where(visible, score, -1e30), axis=2))
    weight = jnp.where(visible, jnp.exp(score - new_top[..., None]), 0.0)
    factor = jnp.exp(top - new_top)
    total = total * factor + jnp.sum(weight, axis=2)
    accum = accum * factor[..., None] + jnp.einsum(
        "tgn,nd->tgd", weight.astype(jnp.bfloat16), values, preferred_element_type=jnp.float32
    )
    return (new_top, total, accum)


def body(activations, queries, w_kv, span_of, mesh=None):
    factors = plan(mesh, activations.shape[0], w_kv.shape[0], w_kv.shape[1], queries.shape[2])
    if factors is not None:
        return fused(factors, activations, queries, w_kv, span_of)
    tokens = activations.shape[0]
    head_dim = queries.shape[2]
    half = tokens // 2
    scale = 1.0 / math.sqrt(head_dim)
    whole = lax.all_gather(activations, "dp", axis=1, tiled=True)
    shard_rows = w_kv.shape[0]
    mine = lax.all_to_all(w_kv, "dp", split_axis=1, concat_axis=0, tiled=True)
    ordered = whole.reshape(tokens, lax.axis_size("dp"), lax.axis_size("ctx"), shard_rows)
    ordered = jnp.transpose(ordered, (0, 2, 1, 3)).reshape(tokens, -1)
    piece = lax.all_gather(mine, "ctx", axis=0, tiled=True)
    count = piece.shape[0]
    projected = jnp.dot(ordered, piece.reshape(count, -1), preferred_element_type=jnp.float32)
    key_value = projected.astype(jnp.bfloat16).reshape(tokens, 2, head_dim)
    all_spans = lax.all_gather(span_of, "ctx", axis=0, tiled=True)
    offsets = jnp.arange(tokens, dtype=jnp.int32)
    own_pos = jnp.where(offsets < half, span_of[0], span_of[1]) * half + offsets % half

    def update(state, part, part_pos):
        return attend(state, part[:, 0], part[:, 1], part_pos, queries, own_pos, scale)

    group = queries.shape[1]
    start_state = (
        jnp.full((tokens, group), -1e30, jnp.float32),
        jnp.zeros((tokens, group), jnp.float32),
        jnp.zeros((tokens, group, head_dim), jnp.float32),
    )
    state = start_state
    piece = lax.all_gather(key_value, "ctx", axis=0, tiled=True)
    count = piece.shape[0]
    index = jnp.arange(count, dtype=jnp.int32)
    key_pos = jnp.take(all_spans, index // half) * half + index % half
    block = 1024 if count % 1024 == 0 else count

    def step(held, item):
        return (update(held, item[0], item[1]), None)

    blocks = (
        piece.reshape(count // block, block, 2, head_dim),
        key_pos.reshape(count // block, block),
    )
    state, _ = lax.scan(step, state, blocks)
    top, total, accum = state
    return (accum / total[..., None]).astype(jnp.bfloat16).reshape(tokens, group * head_dim)


def solution(mesh):
    return jax.shard_map(
        functools.partial(body, mesh=mesh),
        mesh=mesh,
        in_specs=(
            P("ctx", "dp"),
            P("ctx", "dp", None),
            P(("dp", "ctx"), None, None, None),
            P("ctx"),
        ),
        out_specs=P("ctx", "dp"),
        check_vma=False,
    )
```

```python
import functools
import math

import jax
import jax.numpy as jnp
from jax import lax
from jax.experimental import pallas as pl
from jax.experimental.pallas import tpu as pltpu
from jax.sharding import PartitionSpec as P

MESH = pl.DeviceIdType.MESH
VALUE_PART = jnp.bfloat16
STEPS = 32767.0
ORDERS = ((('z', 1), ('x', 1), ('x', 0), ('z', 2), ('w', 0), ('z', 3), ('w', 1), ('x', 3), ('x', 2)), (('z', 1), ('x', 0), ('w', 0), ('z', 3), ('z', 2), ('x', 1), ('w', 1), ('x', 2), ('x', 3)), (('z', 2), ('z', 1), ('x', 0), ('w', 0), ('z', 3), ('x', 1), ('w', 1), ('x', 2), ('x', 3)), (('z', 1), ('x', 0), ('z', 2), ('w', 0), ('z', 3), ('x', 1), ('w', 1), ('x', 2), ('x', 3)))
FIRST = (('line', 1), ('line', 2), ('line', 3), ('both', 1), ('both', 2), ('core', 0), ('both', 3), ('x', 0))
GATHER = (('line', 3), ('over', 3), ('over', 2), ('line', 2), ('line', 1), ('over', 0), ('over', 1))
KEYS = (1, 2, 3)
VALUES = (1, 2, 3)


def remote(src, dst, send, recv, dp, ctx):
    return pltpu.make_async_remote_copy(
        src_ref=src,
        dst_ref=dst,
        send_sem=send,
        recv_sem=recv,
        device_id={"dp": dp, "ctx": ctx},
        device_id_type=MESH,
    )


def fused_kernel(
    X, C, Z, G, scale,
    a_hbm, q_in, w_hbm, span_in, o_ref,
    q_ref, w_in, wloc, abuf, wbuf, psum_k, psum_v, got_k, got_v, rsum, rgot, kbuf, vbuf, spbuf, bias,
    send_sem, a_sem, w_sem, p_sem, r_sem, g_sem, s_sem, own_sem, span_ref, a_ref,
):
    dp, ctx = lax.axis_index("dp"), lax.axis_index("ctx")
    x, c = lax.div(dp, C), lax.rem(dp, C)
    z, y = lax.div(ctx, G), lax.rem(ctx, G)
    tokens = a_ref.shape[0]
    half = tokens // 2
    fw, hd = abuf.shape[3], kbuf.shape[2]
    heads = w_in.shape[1]
    psum, got, outs = (psum_k, psum_v), (got_k, got_v), (kbuf, vbuf)
    xo, co, yo = X - 1 - x, C - 1 - c, G - 1 - y
    across, beside, corner = xo * C + c, x * C + co, xo * C + co

    way = 1 - 2 * lax.div(2 * z, Z)
    edge = (z == 0) | (z == Z - 1)
    line = [z, z + way, jnp.where(edge, z + 2 * way, z - way), jnp.where(edge, z + 3 * way, z + 2 * way)]

    def arrived(slot, recv):
        remote(slot, slot, recv, recv, dp, ctx).wait_recv()

    sent = {}

    def send(src, dst, recv, to_dp, to_ctx, want=None, name=None):
        key = len(sent) if name is None else name
        n = sent.setdefault(key, (len(sent), want, (tuple(src.shape), jnp.dtype(src.dtype))))[0]
        copy = remote(src, dst, send_sem.at[n], recv, to_dp, to_ctx)
        if want is None:
            copy.start()
        else:
            pl.when(want)(copy.start)

    def send_if(want, *args, **kwargs):
        send(*args, want=want, **kwargs)

    peers = [(dp, line[k] * G + y) for k in range(1, Z)]
    peers += [(dp, line[k] * G + yo) for k in range(Z)]
    peers += [(beside, z * G + yo), (across, ctx), (beside, ctx), (corner, ctx)]
    peers += [(across, line[k] * G + y) for k in range(1, Z)]

    def skips(source, target):
        return (jnp.abs(source - target) == Z - 1) | ((jnp.abs(source - target) == 1) & (source + target != Z - 1))

    load_w = pltpu.make_async_copy(w_hbm, w_in, own_sem.at[2])
    load_q = pltpu.make_async_copy(q_in, q_ref, own_sem.at[3])
    load_a = pltpu.make_async_copy(a_hbm, a_ref, own_sem.at[4])
    barrier = pltpu.get_barrier_semaphore()
    for pd, pc in peers:
        pl.semaphore_signal(barrier, inc=1, device_id={"dp": pd, "ctx": pc}, device_id_type=MESH)
    load_s = pltpu.make_async_copy(span_in, span_ref, own_sem.at[1])
    load_a.start()
    load_w.start()
    load_s.start()
    own_a = a_ref.at[:, pl.ds(pl.multiple_of(z * fw, fw), fw)]
    copy_a = pltpu.make_async_copy(own_a, abuf.at[dp, z], own_sem.at[0])
    load_q.start()
    pl.semaphore_wait(barrier, len(peers))
    load_a.wait()
    copy_a.start()

    for kind, k in FIRST:
        piece = a_ref.at[:, pl.ds(pl.multiple_of(line[k] * fw, fw), fw)]
        if kind == "line":
            send(piece, abuf.at[dp, z], a_sem.at[dp, z], dp, line[k] * G + y)
        elif kind == "both":
            send_if(skips(z, line[k]), piece, abuf.at[dp, z], a_sem.at[dp, z], across, line[k] * G + y)
        else:
            send(piece, abuf.at[dp, z], a_sem.at[dp, z], across if kind == "x" else beside, ctx)
    load_w.wait()
    for i in range(2):
        for h in range(heads):
            wloc[i, h] = w_in[:, h, i, :]
        slot, recv = wbuf.at[i, dp, y], w_sem.at[i, dp, y]
        for h in (across, corner):
            send(wloc.at[i, h], slot, recv, h, ctx)
        for h in (dp, beside):
            send(wloc.at[i, h], slot, recv, h, z * G + yo)
        send(wloc.at[i, beside], slot, recv, beside, ctx)
        wbuf[i, dp, y] = wloc[i, dp]
    load_s.wait()
    spbuf[ctx] = jnp.where(
        lax.broadcasted_iota(jnp.int32, spbuf.shape[1:], 0) == 0, span_ref[0], span_ref[1]
    )
    for k in range(Z):
        if k:
            send(spbuf.at[ctx], spbuf.at[ctx], s_sem.at[ctx], dp, line[k] * G + y)
        send(spbuf.at[ctx], spbuf.at[ctx], s_sem.at[ctx], dp, line[k] * G + yo)

    over = z * G + yo
    needed = [None] + [jnp.logical_not(skips(line[k], z)) for k in range(1, Z)]
    ctx_of = [line[k] * G + y for k in range(Z)]

    def relay_w(i):
        for d, far in ((across, 0), (corner, 1)):
            slot, recv = wbuf.at[i, d, y], w_sem.at[i, d, y]
            arrived(slot, recv)
            send(slot, slot, recv, dp, over, name=("w", i, far))

    def relay_z(k):
        slot, recv = abuf.at[dp, line[k]], a_sem.at[dp, line[k]]
        arrived(slot, recv)
        send_if(needed[k], slot, slot, recv, across, ctx, name=("zx", k))
        send(slot, slot, recv, beside, ctx, name=("zc", k))

    def relay_x(k):
        slot, recv = abuf.at[across, line[k]], a_sem.at[across, line[k]]
        arrived(slot, recv)
        send(slot, slot, recv, beside, ctx, name=("xc", k))

    lanes = rsum.shape[2]
    diagonal = lax.broadcasted_iota(jnp.int32, (tokens, lanes), 0) == lax.broadcasted_iota(jnp.int32, (tokens, lanes), 1)

    def project(i, k):
        rows = [abuf[d, line[k]] for d in range(X * C)]
        held = None
        for d in range(X * C):
            part = jnp.dot(rows[d], wbuf[i, d].reshape(fw, hd), preferred_element_type=jnp.float32)
            held = part if held is None else held + part
        return held

    def share(i, k):
        if i == 0:
            for d in (beside, corner):
                arrived(abuf.at[d, line[k]], a_sem.at[d, line[k]])
        if k:
            part = project(i, k)
            if i == 0:
                peak = jnp.maximum(jnp.max(jnp.abs(part), axis=1, keepdims=True), 1e-30)
                part = jnp.round(part * (STEPS / peak)).astype(jnp.int32)
                peaks = jnp.sum(jnp.where(diagonal, peak, 0.0), axis=0, keepdims=True)
                rsum[line[k]] = jnp.broadcast_to(peaks, rsum.shape[1:])
                send(rsum.at[line[k]], rgot.at[z], r_sem.at[z], dp, line[k] * G + y)
            psum[i][line[k]] = part.astype(psum[i].dtype)
            send(psum[i].at[line[k]], got[i].at[z], p_sem.at[i, z], dp, line[k] * G + y)

    def columns(i):
        arrived(wbuf.at[i, beside, y], w_sem.at[i, beside, y])
        for d in (dp, beside, across, corner):
            arrived(wbuf.at[i, d, yo], w_sem.at[i, d, yo])

    relays = {"z": relay_z, "x": relay_x, "w": relay_w}
    for at_z, steps in enumerate(ORDERS):
        @pl.when(z == at_z)
        def _(steps=steps):
            for kind, k in steps:
                relays[kind](k)

    columns(0)
    for k in KEYS:
        share(0, k)
    columns(1)
    for k in VALUES:
        share(1, k)
    copy_a.wait()
    share(0, 0)
    totals = [project(0, 0), None]

    for k in range(Z):
        if k:
            arrived(spbuf.at[line[k] * G + y], s_sem.at[line[k] * G + y])
        arrived(spbuf.at[line[k] * G + yo], s_sem.at[line[k] * G + yo])
    count = Z * G * tokens
    lane = lax.broadcasted_iota(jnp.int32, (1, count), 1)
    key_pos = jnp.zeros((1, count), jnp.int32)
    lanes = spbuf.shape[2]
    for j in range(Z * G):
        for i in range(2):
            base = j * tokens + i * half
            row = spbuf[j, i:i + 1, :]
            row = jnp.concatenate([row] * (count // lanes), axis=1)
            key_pos = jnp.where((lane >= base) & (lane < base + half), row * half + (lane - base), key_pos)
    at = lax.broadcasted_iota(jnp.int32, (tokens, 1), 0)
    own_pos = jnp.where(at < half, span_ref[0] * half + at, span_ref[1] * half + (at - half))
    bias[...] = jnp.where(key_pos <= own_pos, 0.0, -1e30)

    def straight(source, target):
        return (c == 0) & (((source == 0) & (target == 1)) | (target == 0))

    for i in range(2):
        if i:
            totals[i] = project(i, 0)
        for k in range(1, Z):
            zs = line[k]
            arrived(got[i].at[zs], p_sem.at[i, zs])
            part = got[i][zs].astype(jnp.float32)
            if i == 0:
                arrived(rgot.at[zs], r_sem.at[zs])
                part *= jnp.sum(jnp.where(diagonal, rgot[zs, 0:1, :], 0.0), axis=1, keepdims=True) * (1.0 / STEPS)
            totals[i] += part
        outs[i][ctx] = totals[i].astype(outs[i].dtype)
        mine, recv = outs[i].at[ctx], g_sem.at[i, ctx]
        for kind, k in GATHER:
            if kind == "line":
                send(mine, mine, recv, dp, line[k] * G + y)
            elif k:
                send_if(straight(z, line[k]), mine, mine, recv, dp, line[k] * G + yo)
            else:
                send(mine, mine, recv, dp, z * G + yo)

    def relay(i):
        for k in (3, 2, 1):
            src = line[k] * G + y
            slot, recv = outs[i].at[src], g_sem.at[i, src]
            arrived(slot, recv)
            send_if(jnp.logical_not(straight(line[k], z)), slot, slot, recv, dp, z * G + yo)

    def gathered(i):
        for k in range(Z):
            src = line[k] * G + yo
            arrived(outs[i].at[src], g_sem.at[i, src])

    load_q.wait()
    relay(0)
    relay(1)
    gathered(0)
    keys = outs[0][...].reshape(count, hd)
    weights, norms = [], []
    for g in range(q_ref.shape[1]):
        query = q_ref[:, g, :]
        score = lax.dot_general(query, keys, (((1,), (1,)), ((), ())), preferred_element_type=jnp.float32)
        score = score * scale + bias[...]
        weight = jnp.exp(score - jnp.max(score, axis=1, keepdims=True))
        norms.append(1.0 / jnp.sum(weight, axis=1, keepdims=True))
        weights.append(weight.astype(jnp.bfloat16))
    gathered(1)
    values = outs[1][...].reshape(count, hd)
    for g in range(q_ref.shape[1]):
        mixed = jnp.dot(weights[g], values, preferred_element_type=jnp.float32)
        o_ref[:, g * hd:(g + 1) * hd] = (mixed * norms[g]).astype(o_ref.dtype)

    models = (a_ref.at[:, pl.ds(0, fw)], abuf.at[0, 0], wbuf.at[0, 0, 0], psum_k.at[0], psum_v.at[0],
              rsum.at[0], spbuf.at[0])
    models = {(tuple(m.shape), jnp.dtype(m.dtype)): m for m in models}
    for n, want, kind in sent.values():
        wait = remote(models[kind], models[kind], send_sem.at[n], send_sem.at[n], dp, ctx).wait_send
        if want is None:
            wait()
        else:
            pl.when(want)(wait)


def plan(mesh, tokens, shard_rows, heads, head_dim):
    dp, ctx = mesh.shape["dp"], mesh.shape["ctx"]
    if heads != dp or tokens % 16 or tokens > 128 or shard_rows % 16 or head_dim % 128 or (ctx * tokens) % 128:
        return None
    if dp != 4 or ctx != 8 or (2 * shard_rows) % 128:
        return None
    return dp // 2, 2, ctx // 2, 2


def fused(factors, activations, queries, w_kv, span_of):
    X, C, Z, G = factors
    tokens = activations.shape[0]
    shard_rows, heads, _, hd = w_kv.shape
    fw, ctx, dp = G * shard_rows, Z * G, X * C
    group = queries.shape[1]
    dma = pltpu.SemaphoreType.DMA
    bf16, f32 = jnp.bfloat16, jnp.float32
    block = (tokens, hd)
    hbm = pl.BlockSpec(memory_space=pl.ANY)
    sends = 20 * Z + 40
    return pl.pallas_call(
        functools.partial(fused_kernel, X, C, Z, G, 1.0 / math.sqrt(hd)),
        out_shape=pltpu.VMEM((tokens, group * hd), bf16),
        in_specs=[hbm, hbm, hbm, hbm],
        scratch_shapes=[
            pltpu.VMEM(queries.shape, bf16),
            pltpu.VMEM(w_kv.shape, bf16),
            pltpu.VMEM((2, heads, shard_rows, hd), bf16),
            pltpu.VMEM((dp, Z, tokens, fw), bf16),
            pltpu.VMEM((2, dp, G, shard_rows, hd), bf16),
            pltpu.VMEM((Z, *block), jnp.int16),
            pltpu.VMEM((Z, *block), VALUE_PART),
            pltpu.VMEM((Z, *block), jnp.int16),
            pltpu.VMEM((Z, *block), VALUE_PART),
            pltpu.VMEM((Z, 8, 128), f32),
            pltpu.VMEM((Z, 8, 128), f32),
            pltpu.VMEM((ctx, *block), bf16),
            pltpu.VMEM((ctx, *block), bf16),
            pltpu.VMEM((ctx, 8, 128), jnp.int32),
            pltpu.VMEM((tokens, ctx * tokens), f32),
            dma((sends,)), dma((dp, Z)), dma((2, dp, G)), dma((2, Z)), dma((Z,)), dma((2, ctx)), dma((ctx,)), dma((5,)),
            pltpu.SMEM(span_of.shape, jnp.int32),
            pltpu.VMEM(activations.shape, bf16),
        ],
        compiler_params=pltpu.CompilerParams(collective_id=0, has_side_effects=True),
        name="fused",
    )(
        activations,
        queries,
        w_kv,
        span_of,
    )


def attend(carry, keys, values, key_pos, query, query_pos, scale):
    top, total, accum = carry
    score = jnp.einsum("tgd,nd->tgn", query, keys, preferred_element_type=jnp.float32) * scale
    visible = (key_pos[None, :] <= query_pos[:, None])[:, None, :]
    new_top = jnp.maximum(top, jnp.max(jnp.where(visible, score, -1e30), axis=2))
    weight = jnp.where(visible, jnp.exp(score - new_top[..., None]), 0.0)
    factor = jnp.exp(top - new_top)
    total = total * factor + jnp.sum(weight, axis=2)
    accum = accum * factor[..., None] + jnp.einsum(
        "tgn,nd->tgd", weight.astype(jnp.bfloat16), values, preferred_element_type=jnp.float32
    )
    return (new_top, total, accum)


def body(activations, queries, w_kv, span_of, mesh=None):
    factors = plan(mesh, activations.shape[0], w_kv.shape[0], w_kv.shape[1], queries.shape[2])
    if factors is not None:
        return fused(factors, activations, queries, w_kv, span_of)
    tokens = activations.shape[0]
    head_dim = queries.shape[2]
    half = tokens // 2
    scale = 1.0 / math.sqrt(head_dim)
    whole = lax.all_gather(activations, "dp", axis=1, tiled=True)
    shard_rows = w_kv.shape[0]
    mine = lax.all_to_all(w_kv, "dp", split_axis=1, concat_axis=0, tiled=True)
    ordered = whole.reshape(tokens, lax.axis_size("dp"), lax.axis_size("ctx"), shard_rows)
    ordered = jnp.transpose(ordered, (0, 2, 1, 3)).reshape(tokens, -1)
    piece = lax.all_gather(mine, "ctx", axis=0, tiled=True)
    count = piece.shape[0]
    projected = jnp.dot(ordered, piece.reshape(count, -1), preferred_element_type=jnp.float32)
    key_value = projected.astype(jnp.bfloat16).reshape(tokens, 2, head_dim)
    all_spans = lax.all_gather(span_of, "ctx", axis=0, tiled=True)
    offsets = jnp.arange(tokens, dtype=jnp.int32)
    own_pos = jnp.where(offsets < half, span_of[0], span_of[1]) * half + offsets % half

    def update(state, part, part_pos):
        return attend(state, part[:, 0], part[:, 1], part_pos, queries, own_pos, scale)

    group = queries.shape[1]
    start_state = (
        jnp.full((tokens, group), -1e30, jnp.float32),
        jnp.zeros((tokens, group), jnp.float32),
        jnp.zeros((tokens, group, head_dim), jnp.float32),
    )
    state = start_state
    piece = lax.all_gather(key_value, "ctx", axis=0, tiled=True)
    count = piece.shape[0]
    index = jnp.arange(count, dtype=jnp.int32)
    key_pos = jnp.take(all_spans, index // half) * half + index % half
    block = 1024 if count % 1024 == 0 else count

    def step(held, item):
        return (update(held, item[0], item[1]), None)

    blocks = (
        piece.reshape(count // block, block, 2, head_dim),
        key_pos.reshape(count // block, block),
    )
    state, _ = lax.scan(step, state, blocks)
    top, total, accum = state
    return (accum / total[..., None]).astype(jnp.bfloat16).reshape(tokens, group * head_dim)


def solution(mesh):
    return jax.shard_map(
        functools.partial(body, mesh=mesh),
        mesh=mesh,
        in_specs=(
            P("ctx", "dp"),
            P("ctx", "dp", None),
            P(("dp", "ctx"), None, None, None),
            P("ctx"),
        ),
        out_specs=P("ctx", "dp"),
        check_vma=False,
    )
```
